32 devices in a mesh: lat: 4 (over x, core), lon: 8 (over z, y).
Axes of the slice: x: 2, y: 2, z: 4, core: 2. Of those that a mesh axis runs over, the one named last changes fastest.
Arguments:
- fine_tokens: bfloat16 [2, 48, 96, 512], P(None, 'lat', 'lon'), may hold values from -6 to 6
- qkv_weight: bfloat16 [512, 1536], P(None, 'lat'), may hold values from -2 to 2
- proj_weight: bfloat16 [512, 512], P(None, 'lat'), may hold values from -0.25 to 0.25
- merge_one: bfloat16 [2048, 1024], P(None, 'lat'), may hold values from -0.125 to 0.125
- merge_two: bfloat16 [4096, 2048], P('lon'), may hold values from -0.09375 to 0.09375
- mlp_in: bfloat16 [2048, 8192], P(None, 'lon'), may hold values from -0.125 to 0.125
- mlp_out: bfloat16 [8192, 2048], P('lon'), may hold values from -0.125 to 0.125
- split_weight: bfloat16 [2048, 4096], P(None, 'lon'), may hold values from -0.125 to 0.125
Outputs:
- fine_out: float32 [2, 48, 96, 512], P(None, 'lat', 'lon')
- mid_out: float32 [2, 24, 48, 1024], P(None, 'lat', 'lon')
The draws below stay inside these ranges and needn't reach their ends.
All inputs are finite; a program needn't handle non-finite values.
Results may differ from the reference program's by a relative error of at most 0.029.
Values may be sent and summed in bfloat16 or wider, within the bound.
A program may use at most 64 MiB of HBM per device.

```python
import math
import jax
import jax.numpy as jnp
from jax import lax

D = 512
MID = 1024
TOP = 2048
EXPAND = 8192
HEADS = 8
LEV = 2
WIN_R = 6
WIN_C = 12
SHIFT_R = 3
SHIFT_C = 6
NR = 48
NC = 96
N_LON = 8


def draw_qkv_weight(key, part):
    values = jax.random.normal(key, (D, 3 * D), jnp.float32) / math.sqrt(D)
    return jnp.clip(values, -2.0, 2.0).astype(jnp.bfloat16)


def levels(key, extent, cuts, smallest, largest):
    gain, own = 1.0, jax.random.fold_in(key, 6)
    for dim, blocks in cuts:
        heights = jnp.exp(jax.random.uniform(jax.random.fold_in(own, dim), (blocks,), jnp.float32, smallest / len(cuts), largest / len(cuts)))
        gain = gain * jnp.repeat(heights, extent[dim] // blocks).reshape([-1 if axis == dim else 1 for axis in range(len(extent))])
    return gain


def normal_values(rng, dims, scale, most, split=(), held_as=jnp.bfloat16):
    drawn = jax.random.normal(rng, dims, jnp.float32) * scale
    if len(split) > 0:
        drawn = levels(rng, dims, split, -0.22, 0.18) * drawn
    return jnp.clip(drawn, min=-most, max=most).astype(held_as)


def setup_inputs(seed: int = 0) -> dict:
    streams_of = jax.random.split(jax.random.key(seed), 9)
    fine_tokens = normal_values(streams_of[0], (LEV, NR, NC, D), 1.0, 6.0, ((1, 4), (2, 8)))
    qkv_weight = draw_qkv_weight(jax.random.fold_in(streams_of[8], 71), 0)
    proj_weight = normal_values(streams_of[2], (D, D), D ** -0.5, 0.25, ((1, 4),))
    merge_one = normal_values(streams_of[3], (4 * D, MID), (4 * D) ** -0.5, 0.125, ((1, 4),))
    merge_two = normal_values(streams_of[4], (4 * MID, TOP), (4 * MID) ** -0.5, 0.09375, ((0, 8),))
    mlp_in = normal_values(streams_of[5], (TOP, EXPAND), TOP ** -0.5, 0.125, ((1, 8),))
    mlp_out = normal_values(streams_of[6], (EXPAND, TOP), (EXPAND // 4) ** -0.5, 0.125, ((0, 8),))
    split_weight = normal_values(streams_of[7], (TOP, 4 * MID), TOP ** -0.5, 0.125, ((1, 8),))
    return {"fine_tokens": fine_tokens, "qkv_weight": qkv_weight, "proj_weight": proj_weight, "merge_one": merge_one, "merge_two": merge_two, "mlp_in": mlp_in, "mlp_out": mlp_out, "split_weight": split_weight}


def layer_norm(values):
    centre = lax.optimization_barrier(jnp.mean(values, axis=-1, keepdims=True))
    shifted = values - centre
    spread = lax.optimization_barrier(jnp.mean(shifted * shifted, axis=-1, keepdims=True))
    return shifted * lax.rsqrt(spread + 1e-05)

def attend_group(qkv_group, row_index):
    wins = NC // WIN_C
    tokens = LEV * WIN_R * WIN_C
    head_dim = D // HEADS
    parts = qkv_group.reshape(LEV, WIN_R, wins, WIN_C, 3, HEADS, head_dim)
    parts = parts.transpose(2, 0, 1, 3, 4, 5, 6).reshape(wins, tokens, 3, HEADS, head_dim)
    query = parts[:, :, 0].astype(jnp.float32)
    keys = parts[:, :, 1].astype(jnp.float32)
    values = parts[:, :, 2].astype(jnp.float32)
    scores = jnp.einsum('wqhd,wkhd->whqk', query, keys) / math.sqrt(head_dim)
    wrapped = (row_index >= NR - SHIFT_R).astype(jnp.int32)
    labels = jnp.broadcast_to(wrapped[None, :, None], (LEV, WIN_R, WIN_C)).reshape(tokens)
    allowed = labels[:, None] == labels[None, :]
    scores = jnp.where(allowed[None, None], scores, jnp.float32(-1000000000.0))
    top = lax.optimization_barrier(jnp.max(scores, axis=-1, keepdims=True))
    expo = jnp.exp(scores - top)
    probs = (expo / lax.optimization_barrier(jnp.sum(expo, axis=-1, keepdims=True))).astype(jnp.bfloat16)
    heads_out = jnp.einsum('whqk,wkhd->wqhd', probs.astype(jnp.float32), values).astype(jnp.bfloat16)
    heads_out = heads_out.reshape(wins, LEV, WIN_R, WIN_C, D).transpose(1, 2, 0, 3, 4)
    return heads_out.reshape(LEV, WIN_R, NC, D)

def cat_four(grid):
    lev, rows, cols, width = grid.shape
    grid = grid.reshape(lev, rows // 2, 2, cols // 2, 2, width).transpose(0, 1, 3, 2, 4, 5)
    return grid.reshape(lev, rows // 2, cols // 2, 4 * width)

def reference(fine_tokens, qkv_weight, proj_weight, merge_one, merge_two, mlp_in, mlp_out, split_weight):
    moved = jnp.roll(fine_tokens, (-SHIFT_R, -SHIFT_C), axis=(1, 2))
    normed = layer_norm(moved.astype(jnp.float32)).astype(jnp.bfloat16).reshape(-1, D)
    qkv = jnp.dot(normed, qkv_weight, preferred_element_type=jnp.float32).astype(jnp.bfloat16)
    groups = NR // WIN_R
    qkv = qkv.reshape(LEV, groups, WIN_R, NC, 3 * D).transpose(1, 0, 2, 3, 4)
    row_ids = jnp.arange(NR, dtype=jnp.int32).reshape(groups, WIN_R)
    heads_out = lax.map(lambda pair: attend_group(pair[0], pair[1]), (qkv, row_ids))
    heads_out = heads_out.transpose(1, 0, 2, 3, 4).reshape(-1, D)
    attn = jnp.dot(heads_out, proj_weight, preferred_element_type=jnp.float32).astype(jnp.bfloat16)
    attn = attn.reshape(LEV, NR, NC, D)
    fine_out = fine_tokens.astype(jnp.float32) + jnp.roll(attn, (SHIFT_R, SHIFT_C), axis=(1, 2)).astype(jnp.float32)
    cat1 = layer_norm(cat_four(fine_out)).astype(jnp.bfloat16)
    merged1 = jnp.dot(cat1.reshape(-1, 4 * D), merge_one, preferred_element_type=jnp.float32).astype(jnp.bfloat16)
    merged1 = merged1.reshape(LEV, NR // 2, NC // 2, MID)
    normed2 = layer_norm(cat_four(merged1.astype(jnp.float32))).astype(jnp.bfloat16).reshape(-1, 4 * MID)
    count = normed2.shape[0]
    block = 4 * MID // N_LON

    def merge_step(index, total):
        piece = lax.dynamic_slice_in_dim(normed2, index * block, block, 1)
        rows = lax.dynamic_slice_in_dim(merge_two, index * block, block, 0)
        term = jnp.dot(piece, rows, preferred_element_type=jnp.float32).astype(jnp.bfloat16)
        return total + term.astype(jnp.float32)
    merged2 = lax.fori_loop(0, N_LON, merge_step, jnp.zeros((count, TOP), jnp.float32))
    normed3 = layer_norm(merged2).astype(jnp.bfloat16)
    hidden_block = EXPAND // N_LON

    def mlp_step(index, total):
        cols_in = lax.dynamic_slice_in_dim(mlp_in, index * hidden_block, hidden_block, 1)
        rows_out = lax.dynamic_slice_in_dim(mlp_out, index * hidden_block, hidden_block, 0)
        act = jax.nn.gelu(jnp.dot(normed3, cols_in, preferred_element_type=jnp.float32)).astype(jnp.bfloat16)
        term = jnp.dot(act, rows_out, preferred_element_type=jnp.float32).astype(jnp.bfloat16)
        return total + term.astype(jnp.float32)
    mlp = lax.fori_loop(0, N_LON, mlp_step, jnp.zeros((count, TOP), jnp.float32))
    coarse = (merged2 + mlp).astype(jnp.bfloat16)
    pieces = jnp.dot(coarse, split_weight, preferred_element_type=jnp.float32).astype(jnp.bfloat16)
    pieces = pieces.reshape(LEV, NR // 4, NC // 4, 2, 2, MID).transpose(0, 1, 3, 2, 4, 5)
    pieces = pieces.reshape(LEV, NR // 2, NC // 2, MID)
    mid_out = merged1.astype(jnp.float32) + pieces.astype(jnp.float32)
    return (fine_out, mid_out)
```

```python
import functools
import math

import jax
import jax.numpy as jnp
from jax import lax
from jax.experimental import pallas as pl
from jax.experimental.pallas import tpu as pltpu
from jax.sharding import PartitionSpec as P

MID = 1024
HEADS = 8
WIN_R = 6
WIN_C = 12
SHIFT_R = 3
SHIFT_C = 6


def layer_norm(values):
    centre = jnp.mean(values, axis=-1, keepdims=True)
    shifted = values - centre
    spread = jnp.mean(shifted * shifted, axis=-1, keepdims=True)
    return shifted * lax.rsqrt(spread + 1e-05)


def cat_four(grid):
    lev, rows, cols, width = grid.shape
    grid = grid.reshape(lev, rows // 2, 2, cols // 2, 2, width).transpose(0, 1, 3, 2, 4, 5)
    return grid.reshape(lev * (rows // 2) * (cols // 2), 4 * width)


def coarse_kernel(
    blocks_ref, two_hbm, in_hbm, out_hbm, split_hbm, pieces_ref,
    two, w_in, w_out, split, landed, features, sent, summed, own, gathered, normed, act,
    sent2, summed2, gathered2, cols, sent3, landed3,
    load_sem, send_sem, recv_sem, relay_send, relay_recv,
):
    count = lax.axis_size("lon")
    me = lax.axis_index("lon")
    own_count = blocks_ref.shape[1]
    width = own.shape[1]
    loads = [
        pltpu.make_async_copy(source, target, load_sem.at[index])
        for index, (source, target) in enumerate(
            ((two_hbm, two), (in_hbm, w_in), (out_hbm, w_out), (split_hbm, split))
        )
    ]
    for load in loads:
        load.start()
    barrier = pltpu.get_barrier_semaphore()

    def greet(step, carry):
        peer = lax.rem(me + step, count)
        pl.semaphore_signal(
            barrier, inc=1, device_id={"lon": peer}, device_id_type=pl.DeviceIdType.MESH
        )
        return carry

    lax.fori_loop(1, count, greet, 0)
    pl.semaphore_wait(barrier, count - 1)

    def copy_to(phase, peer, source, target):
        return pltpu.make_async_remote_copy(
            src_ref=source,
            dst_ref=target.at[me],
            send_sem=send_sem.at[phase, peer],
            recv_sem=recv_sem.at[phase, me],
            device_id={"lon": peer},
            device_id_type=pl.DeviceIdType.MESH,
        )

    def wait_from(phase, target):
        def body(step, carry):
            peer = lax.rem(me + step, count)
            pltpu.make_async_remote_copy(
                src_ref=target.at[peer],
                dst_ref=target.at[peer],
                send_sem=send_sem.at[phase, peer],
                recv_sem=recv_sem.at[phase, peer],
                device_id={"lon": peer},
                device_id_type=pl.DeviceIdType.MESH,
            ).wait_recv()
            return carry

        lax.fori_loop(1, count, body, 0)

    def wait_sent(phase, source_of, target):
        def body(step, carry):
            peer = lax.rem(me + step, count)
            copy_to(phase, peer, source_of(peer), target).wait_send()
            return carry

        lax.fori_loop(1, count, body, 0)

    def scatter_products(phase, left, weight, send, target):
        def product(peer):
            cut = pl.ds(pl.multiple_of(peer * width, width), width)
            return jnp.dot(left[...], weight[:, cut], preferred_element_type=jnp.float32)

        def body(step, carry):
            peer = lax.rem(me + step, count)
            send[peer] = product(peer).astype(jnp.bfloat16)
            copy_to(phase, peer, send.at[peer], target).start()
            return carry

        lax.fori_loop(1, count, body, 0)
        total = product(me)
        wait_from(phase, target)

        def add(step, total):
            return total + target[lax.rem(me + step, count)].astype(jnp.float32)

        return lax.fori_loop(1, count, add, total)

    chips = count // 2
    z, y = me // 2, lax.rem(me, 2)
    partner = me + 1 - 2 * y
    up, down, over = 0, 1, 2

    def hop(source, target, sent_sem, came_sem, peer):
        return pltpu.make_async_remote_copy(
            src_ref=source,
            dst_ref=target,
            send_sem=sent_sem,
            recv_sem=came_sem,
            device_id={"lon": peer},
            device_id_type=pl.DeviceIdType.MESH,
        )

    def relay(phase, target, kind, block, peer):
        return hop(
            target.at[block],
            target.at[block],
            relay_send.at[phase, kind, block],
            relay_recv.at[phase, block],
            peer,
        )

    def relays(phase, target, act_on, arriving):
        pl.when(z < chips - 1)(lambda: act_on(relay(phase, target, up, me, me + 2)))
        pl.when(z > 0)(lambda: act_on(relay(phase, target, down, me, me - 2)))
        act_on(relay(phase, target, over, me, partner))
        for far in range(1, chips):

            @pl.when(z - far >= 0)
            def _():
                block = me - 2 * far
                if arriving:
                    relay(phase, target, up, block, me - 2).wait_recv()
                pl.when(z < chips - 1)(
                    lambda: act_on(relay(phase, target, up, block, me + 2))
                )
                act_on(relay(phase, target, over, block, partner))

            @pl.when(z + far < chips)
            def _():
                block = me + 2 * far
                if arriving:
                    relay(phase, target, down, block, me + 2).wait_recv()
                pl.when(z > 0)(lambda: act_on(relay(phase, target, down, block, me - 2)))
                act_on(relay(phase, target, over, block, partner))

    def gather(phase, target):
        relays(phase, target, lambda copy: copy.start(), True)
        for row in range(chips):
            relay(phase, target, over, 2 * row + 1 - y, partner).wait_recv()

    def wait_gather(phase, target):
        relays(phase, target, lambda copy: copy.wait_send(), False)

    def first(step, carry):
        peer = lax.rem(me + step, count)
        copy_to(0, peer, blocks_ref.at[peer], landed).start()
        return carry

    lax.fori_loop(1, count, first, 0)
    landed[me] = blocks_ref[me]
    wait_from(0, landed)
    for index in range(count):
        features[index * own_count : (index + 1) * own_count] = landed[index].astype(jnp.float32)
    normed[:, : features.shape[1]] = features[...].astype(jnp.bfloat16)
    loads[0].wait()
    merged = scatter_products(1, normed.at[:, : features.shape[1]], two, sent, summed)
    own[...] = merged
    gathered[me] = merged.astype(jnp.bfloat16)
    gather(0, gathered)

    total_width = count * width
    centre = gathered[0].astype(jnp.float32).sum(axis=-1, keepdims=True)
    for index in range(1, count):
        centre += gathered[index].astype(jnp.float32).sum(axis=-1, keepdims=True)
    centre = centre / total_width
    spread = jnp.zeros_like(centre)
    for index in range(count):
        shifted = gathered[index].astype(jnp.float32) - centre
        spread += (shifted * shifted).sum(axis=-1, keepdims=True)
    scale = lax.rsqrt(spread / total_width + 1e-05)
    for index in range(count):
        shifted = gathered[index].astype(jnp.float32) - centre
        normed[:, index * width : (index + 1) * width] = (shifted * scale).astype(jnp.bfloat16)
    loads[1].wait()

    tile = min(256, act.shape[1])

    def hidden(index, carry):
        cut = pl.ds(pl.multiple_of(index * tile, tile), tile)
        values = jnp.dot(normed[...], w_in[:, cut], preferred_element_type=jnp.float32)
        act[:, cut] = jax.nn.gelu(values).astype(jnp.bfloat16)
        return carry

    lax.fori_loop(0, act.shape[1] // tile, hidden, 0)
    loads[2].wait()
    mlp = scatter_products(3, act, w_out, sent2, summed2)
    gathered2[me] = (own[...] + mlp).astype(jnp.bfloat16)
    gather(1, gathered2)
    for index in range(count):
        normed[:, index * width : (index + 1) * width] = gathered2[index]
    loads[3].wait()
    cols[...] = jnp.dot(normed[...], split[...], preferred_element_type=jnp.float32)
    for index in range(count):
        sent3[index] = cols[index * own_count : (index + 1) * own_count].astype(jnp.bfloat16)

    def last(step, carry):
        peer = lax.rem(me + step, count)
        copy_to(5, peer, sent3.at[peer], landed3).start()
        return carry

    lax.fori_loop(1, count, last, 0)
    landed3[me] = sent3[me]
    wait_from(5, landed3)
    pieces_ref[...] = landed3[...]
    wait_sent(0, lambda peer: blocks_ref.at[peer], landed)
    wait_sent(1, lambda peer: sent.at[peer], summed)
    wait_gather(0, gathered)
    wait_sent(3, lambda peer: sent2.at[peer], summed2)
    wait_gather(1, gathered2)
    wait_sent(5, lambda peer: sent3.at[peer], landed3)


def coarse_in_one(blocks, merge_two, mlp_in, mlp_out, split_weight):
    count, own_count, depth = blocks.shape
    tokens, top = count * own_count, merge_two.shape[1]
    width, hidden, split_width = top // count, mlp_in.shape[1], split_weight.shape[1]
    low = jnp.bfloat16
    whole = pl.BlockSpec(memory_space=pltpu.VMEM)
    apart = pl.BlockSpec(memory_space=pl.ANY)
    return pl.pallas_call(
        coarse_kernel,
        out_shape=jax.ShapeDtypeStruct((count, own_count, split_width), low),
        in_specs=[whole, apart, apart, apart, apart],
        out_specs=whole,
        scratch_shapes=[
            pltpu.VMEM(merge_two.shape, low),
            pltpu.VMEM(mlp_in.shape, low),
            pltpu.VMEM(mlp_out.shape, low),
            pltpu.VMEM(split_weight.shape, low),
            pltpu.VMEM((count, own_count, depth), low),
            pltpu.VMEM((tokens, depth), jnp.float32),
            pltpu.VMEM((count, tokens, width), low),
            pltpu.VMEM((count, tokens, width), low),
            pltpu.VMEM((tokens, width), jnp.float32),
            pltpu.VMEM((count, tokens, width), low),
            pltpu.VMEM((tokens, top), low),
            pltpu.VMEM((tokens, hidden), low),
            pltpu.VMEM((count, tokens, width), low),
            pltpu.VMEM((count, tokens, width), low),
            pltpu.VMEM((count, tokens, width), low),
            pltpu.VMEM((tokens, split_width), jnp.float32),
            pltpu.VMEM((count, own_count, split_width), low),
            pltpu.VMEM((count, own_count, split_width), low),
            pltpu.SemaphoreType.DMA((4,)),
            pltpu.SemaphoreType.DMA((6, count)),
            pltpu.SemaphoreType.DMA((6, count)),
            pltpu.SemaphoreType.DMA((2, 3, count)),
            pltpu.SemaphoreType.DMA((2, count)),
        ],
        compiler_params=pltpu.CompilerParams(
            collective_id=0, has_side_effects=True, vmem_limit_bytes=60 * 1024 * 1024
        ),
    )(blocks, merge_two, mlp_in, mlp_out, split_weight)


def coarse_apart(normed2, merge_two, mlp_in, mlp_out, split_weight):
    own_count = normed2.shape[0]
    feature_parts = lax.all_to_all(normed2, "lon", split_axis=1, concat_axis=0, tiled=True)
    partial_value = jnp.dot(feature_parts, merge_two, preferred_element_type=jnp.float32)
    merged2 = lax.psum(partial_value.astype(jnp.bfloat16), "lon").astype(jnp.float32)
    normed3 = layer_norm(merged2).astype(jnp.bfloat16)
    act = jax.nn.gelu(jnp.dot(normed3, mlp_in, preferred_element_type=jnp.float32)).astype(
        jnp.bfloat16
    )
    mlp_own = lax.psum_scatter(
        jnp.dot(act, mlp_out, preferred_element_type=jnp.float32).astype(jnp.bfloat16),
        "lon",
        scatter_dimension=0,
        tiled=True,
    ).astype(jnp.float32)
    own_merged = lax.dynamic_slice_in_dim(merged2, lax.axis_index("lon") * own_count, own_count, 0)
    coarse = (own_merged + mlp_own).astype(jnp.bfloat16)
    split_cols = jnp.dot(
        lax.all_gather(coarse, "lon", axis=0, tiled=True),
        split_weight,
        preferred_element_type=jnp.float32,
    ).astype(jnp.bfloat16)
    return lax.all_to_all(split_cols, "lon", split_axis=0, concat_axis=1, tiled=True)


def halo_kernel(direction, shards, *refs):
    edges, weights = refs[:3], refs[3 : 3 + shards]
    came, wholes = refs[3 + shards : 6 + shards], refs[6 + shards : 6 + 2 * shards]
    edge_send, edge_recv, own_sem, weight_send, weight_recv = refs[6 + 2 * shards :]
    lat_count, lon_count = lax.axis_size("lat"), lax.axis_size("lon")
    row, col = lax.axis_index("lat"), lax.axis_index("lon")
    mesh = pl.DeviceIdType.MESH

    def beside(sign):
        next_row = lax.rem(row + sign + lat_count, lat_count)
        next_col = lax.rem(col + sign + lon_count, lon_count)
        return (next_row, col), (row, next_col), (next_row, next_col)

    other_core = row + 1 - 2 * lax.rem(row, 2)
    other_chip = lax.rem(row + 2, 4)
    side = lax.rem(col, 2)
    pair = col + 1 - 2 * side
    partners = beside(1) + beside(-1)
    if shards:
        partners += ((other_core, col), (other_chip, col), (row, pair))
    barrier = pltpu.get_barrier_semaphore()
    for partner in partners:
        pl.semaphore_signal(barrier, inc=1, device_id=partner, device_id_type=mesh)
    pl.semaphore_wait(barrier, len(partners))

    copies = []
    for index, target in enumerate(beside(direction)):
        copies.append(
            pltpu.make_async_remote_copy(
                src_ref=edges[index],
                dst_ref=came[index],
                send_sem=edge_send.at[index],
                recv_sem=edge_recv.at[index],
                device_id=target,
                device_id_type=mesh,
            )
        )
    for copy in copies:
        copy.start()

    def columns(index, owner):
        width = weights[index].shape[1]
        return wholes[index].at[:, pl.ds(pl.multiple_of(owner * width, width), width)]

    def half(ref, index, which):
        depth = weights[index].shape[0] // 2
        return ref.at[pl.ds(pl.multiple_of(which * depth, depth), depth)]

    def send(index, kind, source, target, device):
        copy = pltpu.make_async_remote_copy(
            src_ref=source,
            dst_ref=target,
            send_sem=weight_send.at[index, kind],
            recv_sem=weight_recv.at[index, kind],
            device_id=device,
            device_id_type=mesh,
        )
        copy.start()
        return copy

    moves = []
    for index in range(shards):
        mine, held = weights[index], columns(index, row)
        away = send(
            index, 0, half(mine, index, side), half(held, index, side), (other_chip, col)
        )
        moves.append([away, send(index, 1, mine, held, (other_core, col))])
        pltpu.make_async_copy(mine, held, own_sem.at[index]).start()
    for index in range(shards):
        moves[index][0].wait_recv()
        part = half(columns(index, other_chip), index, side)
        moves[index].append(send(index, 2, part, part, (row, pair)))
        moves[index].append(send(index, 3, part, part, (other_core, col)))
    for index in range(shards):
        moves[index][2].wait_recv()
        part = half(columns(index, other_chip), index, 1 - side)
        moves[index].append(send(index, 4, part, part, (other_core, col)))
    for index in range(shards):
        away, core, paired, first, second = moves[index]
        for copy in (away, core, paired, first, second):
            copy.wait_send()
        for copy in (core, first, second):
            copy.wait_recv()
        pltpu.make_async_copy(weights[index], columns(index, row), own_sem.at[index]).wait()
    for copy in copies:
        copy.wait()


def exchange(edges, direction, weights, identity):
    whole = pl.BlockSpec(memory_space=pltpu.VMEM)
    shards = len(weights)
    outs = [jax.ShapeDtypeStruct(edge.shape, edge.dtype) for edge in edges]
    outs += [
        jax.ShapeDtypeStruct((part.shape[0], 4 * part.shape[1]), part.dtype) for part in weights
    ]
    return pl.pallas_call(
        functools.partial(halo_kernel, direction, shards),
        out_shape=outs,
        in_specs=[whole] * (3 + shards),
        out_specs=[whole] * (3 + shards),
        scratch_shapes=[
            pltpu.SemaphoreType.DMA((3,)),
            pltpu.SemaphoreType.DMA((3,)),
            pltpu.SemaphoreType.DMA((max(shards, 1),)),
            pltpu.SemaphoreType.DMA((max(shards, 1), 5)),
            pltpu.SemaphoreType.DMA((max(shards, 1), 5)),
        ],
        compiler_params=pltpu.CompilerParams(collective_id=identity, has_side_effects=True),
    )(*edges, *weights)


def lat_swap(value, mask):
    return lax.ppermute(value, "lat", [(index, index ^ mask) for index in range(4)])


def in_owner_order(parts):
    index = lax.axis_index("lat")
    odd, high = index % 2 == 1, index >= 2
    a, b, c, d = parts
    a, b = jnp.where(odd, b, a), jnp.where(odd, a, b)
    c, d = jnp.where(odd, d, c), jnp.where(odd, c, d)
    a, c = jnp.where(high, c, a), jnp.where(high, a, c)
    b, d = jnp.where(high, d, b), jnp.where(high, b, d)
    return jnp.concatenate((a, b, c, d), axis=-1)


def attend_kernel(
    tok, qkv_hbm, proj_hbm, merge_hbm, fine_ref, merged_ref, blocks_ref,
    wq, wp, wm, low, came_row, came_low, packed, normed, qkv, bias, heads, low_back, row_back,
    attn, back_row, back_low, split_fine, cat, cat_low, parts, split_mid, cat2,
    halo_send, halo_recv, own_sem, weight_send, weight_recv,
):
    lat_count, lon_count = lax.axis_size("lat"), lax.axis_size("lon")
    row, col = lax.axis_index("lat"), lax.axis_index("lon")
    mesh = pl.DeviceIdType.MESH
    f32, low_type = jnp.float32, jnp.bfloat16
    rows, slots, width = tok.shape
    levels = 2
    near = levels * SHIFT_C
    edge = low.shape[1]
    head_dim = width // HEADS

    def beside(sign):
        next_row = lax.rem(row + sign + lat_count, lat_count)
        next_col = lax.rem(col + sign + lon_count, lon_count)
        return (next_row, col), (row, next_col), (next_row, next_col)

    other_core = row + 1 - 2 * lax.rem(row, 2)
    other_chip = lax.rem(row + 2, 4)
    far = lax.rem(other_core + 2, 4)
    side = lax.rem(col, 2)
    pair = col + 1 - 2 * side
    low[...] = tok[...].astype(f32)[:, :edge].astype(low_type)
    cat[...] = jnp.zeros_like(cat)
    partners = beside(1) + beside(-1) + ((other_core, col), (other_chip, col), (row, pair))
    barrier = pltpu.get_barrier_semaphore()
    for partner in partners:
        pl.semaphore_signal(barrier, inc=1, device_id=partner, device_id_type=mesh)
    pl.semaphore_wait(barrier, len(partners))

    shards = (qkv_hbm, proj_hbm, merge_hbm)
    counts = WEIGHT_PIECES

    def whole(index, owner):
        if index == 1:
            cut = proj_hbm.shape[1]
            return wp.at[:, pl.ds(pl.multiple_of(owner * cut, cut), cut)]
        return (wq if index == 0 else wm).at[owner]

    def piece(ref, index, which, number):
        depth = shards[index].shape[0] // 2
        size = depth // counts[index]
        start = pl.multiple_of(which * depth + number * size, size)
        return ref.at[pl.ds(start, size)]

    def send(index, kind, number, source, target, device):
        place = kind * max(counts) + number
        copy = pltpu.make_async_remote_copy(
            src_ref=source,
            dst_ref=target,
            send_sem=weight_send.at[index, place],
            recv_sem=weight_recv.at[index, place],
            device_id=device,
            device_id_type=mesh,
        )
        copy.start()
        return copy

    over, across, own = {}, {}, {}
    first, second, third = {}, {}, {}

    def send_over(index):
        for number in range(counts[index]):
            over[index, number] = send(
                index, 0, number,
                piece(shards[index], index, side, number),
                piece(whole(index, row), index, side, number),
                (other_chip, col),
            )

    def send_across(index):
        across[index] = send(
            index, 1, 0, shards[index], whole(index, row), (other_core, col)
        )
        own[index] = pltpu.make_async_copy(shards[index], whole(index, row), own_sem.at[index])
        own[index].start()

    def pass_on(index, number):
        over[index, number].wait_recv()
        held = piece(whole(index, other_chip), index, side, number)
        first[index, number] = send(index, 2, number, held, held, (row, pair))
        second[index, number] = send(index, 3, number, held, held, (other_core, col))

    def pass_last(index, number):
        first[index, number].wait_recv()
        held = piece(whole(index, other_chip), index, 1 - side, number)
        third[index, number] = send(index, 4, number, held, held, (other_core, col))

    def wait_far(index):
        for number in range(counts[index]):
            second[index, number].wait_recv()
            third[index, number].wait_recv()

    def halo(place, source, target, device):
        copy = pltpu.make_async_remote_copy(
            src_ref=source,
            dst_ref=target,
            send_sem=halo_send.at[place],
            recv_sem=halo_recv.at[place],
            device_id=device,
            device_id_type=mesh,
        )
        copy.start()
        return copy

    before, after = beside(-1), beside(1)
    there = [
        halo(0, low.at[SHIFT_R:], came_low.at[SHIFT_R:], before[1]),
        halo(1, low.at[:SHIFT_R], came_low.at[:SHIFT_R], before[2]),
    ]
    send_over(0)
    there.append(halo(2, tok.at[:SHIFT_R], came_row, before[0]))
    send_across(0)
    send_over(1)
    send_across(1)
    send_over(2)
    send_across(2)

    slot = lax.broadcasted_iota(jnp.int32, (1, edge, width), 1)
    tokens = WIN_R * slots
    wins = rows // WIN_R
    key_row = lax.broadcasted_iota(jnp.int32, (tokens, tokens), 1) >= (WIN_R - SHIFT_R) * slots
    query_row = lax.broadcasted_iota(jnp.int32, (tokens, tokens), 0) >= (WIN_R - SHIFT_R) * slots
    last = jnp.where(row == lat_count - 1, f32(-1000000000.0), f32(0.0))
    bias[...] = jnp.where(key_row == query_row, f32(0.0), last)

    for number in range(counts[0]):
        pass_on(0, number)
    for copy in there:
        copy.wait_recv()
    packed[: rows - SHIFT_R] = tok[SHIFT_R:].astype(f32)
    packed[rows - SHIFT_R :] = came_row[...].astype(f32)
    packed[: rows - SHIFT_R, :edge] = jnp.where(
        slot < near, came_low[SHIFT_R:].astype(f32), packed[: rows - SHIFT_R, :edge]
    )
    packed[rows - SHIFT_R :, :edge] = jnp.where(
        slot < near, came_low[:SHIFT_R].astype(f32), packed[rows - SHIFT_R :, :edge]
    )
    for win in range(wins):
        values = packed[win * WIN_R : (win + 1) * WIN_R].reshape(tokens, width)
        normed[win * tokens : (win + 1) * tokens] = layer_norm(values).astype(low_type)

    cut = qkv_hbm.shape[1]

    def project(owner):
        place = pl.ds(pl.multiple_of(owner * cut, cut), cut)
        qkv[:, place] = jnp.dot(
            normed[...], wq[owner], preferred_element_type=f32
        ).astype(low_type)

    own[0].wait()
    project(row)
    across[0].wait_recv()
    project(other_core)
    for number in range(counts[0]):
        pass_last(0, number)
    project(other_chip)
    wait_far(0)
    project(far)

    for number in range(counts[1]):
        pass_on(1, number)
    pass_on(2, 0)

    lane = lax.broadcasted_iota(jnp.int32, (1, 2 * head_dim), 1)
    near_head = jnp.where(lane < head_dim, 1.0, 0.0).astype(low_type)
    scale = 1.0 / math.sqrt(head_dim)

    def attend(win):
        place = pl.ds(win * tokens, tokens)

        def head_pair(index, carry):
            def columns(kind):
                start = pl.multiple_of(kind * width + index * 2 * head_dim, 2 * head_dim)
                return qkv[place, pl.ds(start, 2 * head_dim)]

            query, key, value = columns(0), columns(1), columns(2)
            outs = []
            for mask in (near_head, 1 - near_head):
                scores = lax.dot_general(
                    query, key * mask, (((1,), (1,)), ((), ())), preferred_element_type=f32
                )
                scores = scores * scale
                if win == wins - 1:
                    scores = scores + bias[...]
                expo = jnp.exp(scores - jnp.max(scores, axis=-1, keepdims=True))
                total = jnp.sum(expo, axis=-1, keepdims=True)
                out = jnp.dot(expo.astype(low_type), value, preferred_element_type=f32)
                outs.append(out / total)
            start = pl.multiple_of(index * 2 * head_dim, 2 * head_dim)
            heads[place, pl.ds(start, 2 * head_dim)] = jnp.where(
                lane < head_dim, outs[0], outs[1]
            ).astype(low_type)
            return carry

        lax.fori_loop(0, HEADS // 2, head_pair, 0)

    for win in range(wins):
        attend(win)
        if win == 0:
            for number in range(counts[1]):
                pass_last(1, number)
        pass_on(2, win + 1)
        pass_last(2, win)

    own[1].wait()
    across[1].wait_recv()
    wait_far(1)
    for win in range(wins):
        values = jnp.dot(
            heads[win * tokens : (win + 1) * tokens], wp[...], preferred_element_type=f32
        )
        values = values.astype(low_type).astype(f32).reshape(WIN_R, slots, width)
        attn[win * WIN_R : (win + 1) * WIN_R] = values
    low_back[...] = attn[:, :edge].astype(low_type)
    row_back[...] = attn[rows - SHIFT_R :].astype(low_type)
    kept = rows - SHIFT_R
    back = [
        halo(3, low_back.at[:kept], back_low.at[SHIFT_R:], after[1]),
        halo(4, low_back.at[kept:], back_low.at[:SHIFT_R], after[2]),
        halo(5, row_back, back_row, after[0]),
    ]
    for number in range(wins + 1, counts[2]):
        pass_on(2, number)
    for copy in back:
        copy.wait_recv()

    fine_ref[SHIFT_R:] = tok[SHIFT_R:].astype(f32) + attn[:kept]
    fine_ref[:SHIFT_R] = tok[:SHIFT_R].astype(f32) + back_row[...].astype(f32)
    fine_ref[:, :edge] = jnp.where(
        slot < near,
        tok[...].astype(f32)[:, :edge] + back_low[...].astype(f32),
        fine_ref[:, :edge],
    )

    group = cat.shape[0] // rows
    half_cols = slots // levels // 2
    lanes = 128
    for tile in range(width // lanes):
        split_fine[tile] = fine_ref[:, :, tile * lanes : (tile + 1) * lanes]
    for line in range(rows // 2):
        for level in range(levels):
            for part in range(4):
                start = levels * (part % 2) + level
                base = (line * levels + level) * group
                for tile in range(width // lanes):
                    place = part * width + tile * lanes
                    cat[base : base + half_cols, place : place + lanes] = split_fine[
                        tile, 2 * line + part // 2, pl.ds(start, half_cols, stride=2 * levels), :
                    ]
    for number in range(wins, counts[2]):
        pass_last(2, number)
    cat_low[...] = layer_norm(cat[...]).astype(low_type)
    wide = merge_hbm.shape[1]

    def merge(owner):
        values = jnp.dot(cat_low[...], wm[owner], preferred_element_type=f32)
        place = pl.ds(pl.multiple_of(owner * wide, wide), wide)
        parts[:, place] = values.astype(low_type).astype(f32)

    own[2].wait()
    merge(row)
    across[2].wait_recv()
    merge(other_core)
    merge(other_chip)
    wait_far(2)
    merge(far)
    merged_ref[...] = parts[...].astype(low_type)
    mid = parts.shape[1]
    for tile in range(mid // lanes):
        split_mid[tile] = parts[:, tile * lanes : (tile + 1) * lanes]
    quarter = half_cols // 2
    for line in range(rows // 4):
        for level in range(levels):
            for part in range(4):
                source = ((2 * line + part // 2) * levels + level) * group
                base = (line * levels + level) * quarter
                for tile in range(mid // lanes):
                    place = part * mid + tile * lanes
                    cat2[base : base + quarter, place : place + lanes] = split_mid[
                        tile, pl.ds(source + part % 2, quarter, stride=2), :
                    ]
    values = layer_norm(cat2[...]).astype(low_type)
    count, own_count, depth = blocks_ref.shape
    for index in range(count):
        blocks_ref[index] = values[:, index * depth : (index + 1) * depth]

    for copy in there + back:
        copy.wait_send()
    for copies in (over, across, first, second, third):
        for copy in copies.values():
            copy.wait_send()


WEIGHT_PIECES = (2, 1, 4)


def attend(tokens, qkv_weight, proj_weight, merge_one):
    rows, slots, width = tokens.shape
    low, f32 = jnp.bfloat16, jnp.float32
    levels = slots // (slots // 2)
    count = lax.axis_size("lon")
    near = levels * SHIFT_C
    edge = -(-near // 8) * 8
    half_cols = slots // levels // 2
    group = -(-half_cols // 8) * 8
    cats = rows // 2 * levels * group
    mid = 4 * merge_one.shape[1]
    own_count = rows // 4 * levels * (half_cols // 2)
    whole = pl.BlockSpec(memory_space=pltpu.VMEM)
    apart = pl.BlockSpec(memory_space=pl.ANY)
    tall = rows * slots
    return pl.pallas_call(
        attend_kernel,
        out_shape=[
            jax.ShapeDtypeStruct((rows, slots, width), f32),
            jax.ShapeDtypeStruct((cats, mid), low),
            jax.ShapeDtypeStruct((count, own_count, 4 * mid // count), low),
        ],
        in_specs=[whole, apart, apart, apart],
        out_specs=[whole] * 3,
        scratch_shapes=[
            pltpu.VMEM((4,) + qkv_weight.shape, low),
            pltpu.VMEM((proj_weight.shape[0], 4 * proj_weight.shape[1]), low),
            pltpu.VMEM((4,) + merge_one.shape, low),
            pltpu.VMEM((rows, edge, width), low),
            pltpu.VMEM((SHIFT_R, slots, width), low),
            pltpu.VMEM((rows, edge, width), low),
            pltpu.VMEM((rows, slots, width), f32),
            pltpu.VMEM((tall, width), low),
            pltpu.VMEM((tall, 3 * width), low),
            pltpu.VMEM((WIN_R * slots, WIN_R * slots), f32),
            pltpu.VMEM((tall, width), low),
            pltpu.VMEM((rows, edge, width), low),
            pltpu.VMEM((SHIFT_R, slots, width), low),
            pltpu.VMEM((rows, slots, width), f32),
            pltpu.VMEM((SHIFT_R, slots, width), low),
            pltpu.VMEM((rows, edge, width), low),
            pltpu.VMEM((width // 128, rows, slots, 128), f32),
            pltpu.VMEM((cats, 4 * width), f32),
            pltpu.VMEM((cats, 4 * width), low),
            pltpu.VMEM((cats, mid), f32),
            pltpu.VMEM((mid // 128, cats, 128), f32),
            pltpu.VMEM((own_count, 4 * mid), f32),
            pltpu.SemaphoreType.DMA((6,)),
            pltpu.SemaphoreType.DMA((6,)),
            pltpu.SemaphoreType.DMA((3,)),
            pltpu.SemaphoreType.DMA((3, 5 * max(WEIGHT_PIECES))),
            pltpu.SemaphoreType.DMA((3, 5 * max(WEIGHT_PIECES))),
        ],
        compiler_params=pltpu.CompilerParams(
            collective_id=3, has_side_effects=True, vmem_limit_bytes=40 * 1024 * 1024
        ),
    )(tokens, qkv_weight, proj_weight, merge_one)


def on_any(
    fine_tokens, qkv_weight, proj_weight, merge_one, merge_two, mlp_in, mlp_out, split_weight
):
    levels, rows, cols, width = fine_tokens.shape
    lat_count = lax.axis_size("lat")
    head_dim = width // HEADS
    edges = (
        fine_tokens[:, :SHIFT_R, SHIFT_C:],
        fine_tokens[:, SHIFT_R:, :SHIFT_C],
        fine_tokens[:, :SHIFT_R, :SHIFT_C],
    )
    if lat_count == 4 and lax.axis_size("lon") % 2 == 0:
        row_came, col_came, both_came, full_qkv, full_proj = exchange(
            edges, -1, (qkv_weight, proj_weight), 1
        )
        merge_one, row_came = lax.optimization_barrier((merge_one, row_came))
        merge_far = lat_swap(merge_one, 2)
        merge_parts = (merge_one, lat_swap(merge_one, 1), merge_far, lat_swap(merge_far, 1))
    else:
        row_came, col_came, both_came = exchange(edges, -1, (), 1)
        full_qkv = lax.all_gather(qkv_weight, "lat", axis=1, tiled=True)
        full_proj = lax.all_gather(proj_weight, "lat", axis=1, tiled=True)
    upper = jnp.concatenate([fine_tokens[:, SHIFT_R:, SHIFT_C:], col_came], axis=2)
    lower = jnp.concatenate([row_came, both_came], axis=2)
    moved = jnp.concatenate([upper, lower], axis=1)
    normed = layer_norm(moved.astype(jnp.float32)).astype(jnp.bfloat16).reshape(-1, width)
    qkv = jnp.dot(normed, full_qkv, preferred_element_type=jnp.float32).astype(jnp.bfloat16)
    row_wins = rows // WIN_R
    col_wins = cols // WIN_C
    wins = row_wins * col_wins
    tokens = levels * WIN_R * WIN_C
    parts = qkv.reshape(levels, row_wins, WIN_R, col_wins, WIN_C, 3, HEADS, head_dim)
    parts = parts.transpose(1, 3, 0, 2, 4, 5, 6, 7).reshape(wins, tokens, 3, HEADS, head_dim)
    scores = jnp.einsum(
        "wqhd,wkhd->whqk", parts[:, :, 0], parts[:, :, 1], preferred_element_type=jnp.float32
    )
    scores = scores / math.sqrt(head_dim)
    global_rows = lax.axis_index("lat") * rows + jnp.arange(rows, dtype=jnp.int32)
    wrapped = (global_rows >= rows * lat_count - SHIFT_R).astype(jnp.int32).reshape(row_wins, WIN_R)
    labels = jnp.broadcast_to(
        wrapped[:, None, None, :, None], (row_wins, col_wins, levels, WIN_R, WIN_C)
    )
    labels = labels.reshape(wins, tokens)
    allowed = labels[:, :, None] == labels[:, None, :]
    scores = jnp.where(allowed[:, None], scores, jnp.float32(-1000000000.0))
    top = jnp.max(scores, axis=-1, keepdims=True)
    expo = jnp.exp(scores - top)
    probs = (expo / jnp.sum(expo, axis=-1, keepdims=True)).astype(jnp.bfloat16)
    heads_out = jnp.einsum(
        "whqk,wkhd->wqhd", probs, parts[:, :, 2], preferred_element_type=jnp.float32
    )
    heads_out = heads_out.astype(jnp.bfloat16).reshape(
        row_wins, col_wins, levels, WIN_R, WIN_C, width
    )
    heads_out = heads_out.transpose(2, 0, 3, 1, 4, 5).reshape(-1, width)
    attn = jnp.dot(heads_out, full_proj, preferred_element_type=jnp.float32).astype(jnp.bfloat16)
    attn = attn.reshape(levels, rows, cols, width)
    edges = (
        attn[:, rows - SHIFT_R :, : cols - SHIFT_C],
        attn[:, : rows - SHIFT_R, cols - SHIFT_C :],
        attn[:, rows - SHIFT_R :, cols - SHIFT_C :],
    )
    row_came, col_came, both_came = exchange(edges, 1, (), 2)
    upper = jnp.concatenate([both_came, row_came], axis=2)
    lower = jnp.concatenate([col_came, attn[:, : rows - SHIFT_R, : cols - SHIFT_C]], axis=2)
    back = jnp.concatenate([upper, lower], axis=1)
    fine_out = fine_tokens.astype(jnp.float32) + back.astype(jnp.float32)
    normed1 = layer_norm(cat_four(fine_out)).astype(jnp.bfloat16)
    if lat_count == 4 and lax.axis_size("lon") % 2 == 0:
        merged1 = in_owner_order(
            [
                jnp.dot(normed1, part, preferred_element_type=jnp.float32).astype(jnp.bfloat16)
                for part in merge_parts
            ]
        )
    else:
        merge_all = lax.all_gather(merge_one, "lat", axis=1, tiled=True)
        merged1 = jnp.dot(normed1, merge_all, preferred_element_type=jnp.float32)
        merged1 = merged1.astype(jnp.bfloat16)
    merged1 = merged1.reshape(levels, rows // 2, cols // 2, MID)
    normed2 = layer_norm(cat_four(merged1.astype(jnp.float32))).astype(jnp.bfloat16)
    count = lax.axis_size("lon")
    if count % 2 == 0 and merge_two.shape[1] % (count * 128) == 0:
        blocks = normed2.reshape(normed2.shape[0], count, -1).transpose(1, 0, 2)
        pieces = coarse_in_one(blocks, merge_two, mlp_in, mlp_out, split_weight)
        pieces = pieces.transpose(1, 0, 2)
    else:
        pieces = coarse_apart(normed2, merge_two, mlp_in, mlp_out, split_weight)
    pieces = pieces.reshape(levels, rows // 4, cols // 4, 2, 2, MID).transpose(0, 1, 3, 2, 4, 5)
    pieces = pieces.reshape(levels, rows // 2, cols // 2, MID)
    mid_out = merged1.astype(jnp.float32) + pieces.astype(jnp.float32)
    return (fine_out, mid_out)


def on_device(
    fine_tokens, qkv_weight, proj_weight, merge_one, merge_two, mlp_in, mlp_out, split_weight
):
    levels, rows, cols, width = fine_tokens.shape
    lat_count, count = lax.axis_size("lat"), lax.axis_size("lon")
    fits = count % 2 == 0 and merge_two.shape[1] % (count * 128) == 0
    if lat_count != 4 or not fits or rows != 2 * WIN_R or cols != WIN_C or levels != 2:
        return on_any(
            fine_tokens, qkv_weight, proj_weight, merge_one, merge_two, mlp_in, mlp_out, split_weight
        )
    tokens = fine_tokens.transpose(1, 2, 0, 3).reshape(rows, cols * levels, width)
    fine, merged1, blocks = attend(tokens, qkv_weight, proj_weight, merge_one)
    fine_out = fine.reshape(rows, cols, levels, width).transpose(2, 0, 1, 3)
    pieces = coarse_in_one(blocks, merge_two, mlp_in, mlp_out, split_weight)
    half_rows, half_cols = rows // 2, cols // 2
    pieces = pieces.transpose(1, 0, 2).reshape(rows // 4, levels, cols // 4, 2, 2, MID)
    pieces = pieces.transpose(0, 3, 2, 4, 1, 5).reshape(half_rows, half_cols, levels, MID)
    merged1 = merged1.reshape(half_rows, levels, -1, MID)[:, :, :half_cols].transpose(0, 2, 1, 3)
    mid_out = merged1.astype(jnp.float32) + pieces.astype(jnp.float32)
    return (fine_out, mid_out.transpose(2, 0, 1, 3))


def solution(mesh):
    return jax.shard_map(
        on_device,
        mesh=mesh,
        in_specs=(
            P(None, "lat", "lon", None),
            P(None, "lat"),
            P(None, "lat"),
            P(None, "lat"),
            P("lon", None),
            P(None, "lon"),
            P("lon", None),
            P(None, "lon"),
        ),
        out_specs=(P(None, "lat", "lon", None), P(None, "lat", "lon", None)),
        check_vma=False,
    )
```

```python
import functools
import math

import jax
import jax.numpy as jnp
from jax import lax
from jax.experimental import pallas as pl
from jax.experimental.pallas import tpu as pltpu
from jax.sharding import PartitionSpec as P

MID = 1024
HEADS = 8
WIN_R = 6
WIN_C = 12
SHIFT_R = 3
SHIFT_C = 6


def layer_norm(values):
    centre = jnp.mean(values, axis=-1, keepdims=True)
    shifted = values - centre
    spread = jnp.mean(shifted * shifted, axis=-1, keepdims=True)
    return shifted * lax.rsqrt(spread + 1e-05)


def cat_four(grid):
    lev, rows, cols, width = grid.shape
    grid = grid.reshape(lev, rows // 2, 2, cols // 2, 2, width).transpose(0, 1, 3, 2, 4, 5)
    return grid.reshape(lev * (rows // 2) * (cols // 2), 4 * width)


def coarse_steps(
    blocks_ref, two_hbm, in_hbm, out_hbm, split_hbm, pieces_ref,
    two, w_in, w_out, split, landed, features, feat, y_sent, y_land, z_sent, z_land, held, own,
    gathered, normed, act, cols, sent3,
    load_sem, first_send, first_recv, y_send, y_recv, z_send, z_recv, g_send, g_recv, o_send,
    o_recv, last_send, last_recv, greet,
):
    count = lax.axis_size("lon")
    me = lax.axis_index("lon")
    chips = count // 2
    z, y = me // 2, lax.rem(me, 2)
    partner = me + 1 - 2 * y
    own_count = blocks_ref.shape[1]
    width = own.shape[-1]
    low_type, f32 = jnp.bfloat16, jnp.float32
    loads = [
        pltpu.make_async_copy(source, target, load_sem.at[index])
        for index, (source, target) in enumerate(
            ((two_hbm, two), (in_hbm, w_in), (out_hbm, w_out), (split_hbm, split))
        )
    ]
    for load in loads:
        load.start()
    greet()
    far_first = list(range(2, chips)) + [1] if chips > 2 else list(range(1, chips))

    def level(step):
        return lax.rem(z + step, chips)

    def remote(source, target, sent, came, peer):
        return pltpu.make_async_remote_copy(
            src_ref=source,
            dst_ref=target,
            send_sem=sent,
            recv_sem=came,
            device_id={"lon": peer},
            device_id_type=pl.DeviceIdType.MESH,
        )

    def first_copy(peer, source):
        return remote(
            blocks_ref.at[peer],
            landed.at[lax.rem(source, 2), source // 2],
            first_send.at[peer],
            first_recv.at[source],
            peer,
        )

    def y_copy(phase, chunk, block):
        return remote(
            y_sent.at[phase, chunk, block],
            y_land.at[phase, chunk, block],
            y_send.at[phase, chunk, block],
            y_recv.at[phase, chunk, block],
            partner,
        )

    def z_copy(phase, chunk, to, source):
        return remote(
            z_sent.at[phase, chunk, to],
            z_land.at[phase, chunk, source],
            z_send.at[phase, chunk, to],
            z_recv.at[phase, chunk, source],
            to * 2 + y,
        )

    def g_copy(phase, chunk, to, source):
        place = gathered.at[phase, chunk, source * 2 + y]
        return remote(
            place, place, g_send.at[phase, chunk, to], g_recv.at[phase, chunk, source], to * 2 + y
        )

    def o_copy(phase, chunk, block, side):
        place = gathered.at[phase, chunk, block * 2 + side]
        return remote(
            place, place, o_send.at[phase, chunk, block], o_recv.at[phase, chunk, block], partner
        )

    def last_copy(peer, source):
        return remote(
            sent3.at[lax.rem(peer, 2), peer // 2],
            pieces_ref.at[source],
            last_send.at[peer],
            last_recv.at[source],
            peer,
        )

    def product(left, weight, peer):
        cut = pl.ds(pl.multiple_of(peer * width, width), width)
        return jnp.dot(left[...], weight[:, cut], preferred_element_type=f32)

    def start_y(phase, chunk, left, weight):
        for step in far_first + [0]:
            block = level(step)
            y_sent[phase, chunk, block] = product(left, weight, block * 2 + 1 - y).astype(low_type)
            y_copy(phase, chunk, block).start()

    def hold(chunk, left, weight):
        for step in far_first + [0]:
            block = level(step)
            held[chunk, block] = product(left, weight, block * 2 + y)

    def start_z(phase, chunk):
        for step in far_first:
            block = level(step)
            y_copy(phase, chunk, block).wait_recv()
            total = held[chunk, block] + y_land[phase, chunk, block].astype(f32)
            z_sent[phase, chunk, block] = total.astype(low_type)
            z_copy(phase, chunk, block, z).start()

    def finish(phase, chunk):
        y_copy(phase, chunk, z).wait_recv()
        total = held[chunk, z] + y_land[phase, chunk, z].astype(f32)
        for step in range(1, chips):
            block = level(step)
            z_copy(phase, chunk, block, block).wait_recv()
            total = total + z_land[phase, chunk, block].astype(f32)
        return total

    def spread(phase, chunk, values):
        gathered[phase, chunk, me] = values.astype(low_type)
        for step in far_first:
            g_copy(phase, chunk, level(step), z).start()
        o_copy(phase, chunk, z, y).start()

    def forward(phase, chunk):
        for step in range(1, chips):
            block = level(step)
            g_copy(phase, chunk, block, block).wait_recv()
            o_copy(phase, chunk, block, y).start()

    def arrive(phase, chunk):
        for step in range(chips):
            o_copy(phase, chunk, level(step), 1 - y).wait_recv()

    for step in range(1, count):
        first_copy(lax.rem(me + step, count), me).start()
    landed[y, z] = blocks_ref[me]
    chunks = (0, 1)
    for chunk in chunks:
        for index in range(chips):
            source = index * 2 + chunk
            pl.when(source != me)(lambda: first_copy(source, source).wait_recv())
        for index in range(chips):
            features[index * own_count : (index + 1) * own_count] = landed[chunk, index].astype(f32)
        feat[chunk] = features[...].astype(low_type)
        if chunk == 0:
            loads[0].wait()
        start_y(0, chunk, feat.at[chunk], two)
    for chunk in chunks:
        hold(chunk, feat.at[chunk], two)
        start_z(0, chunk)
    for chunk in chunks:
        merged = finish(0, chunk)
        own[chunk] = merged
        spread(0, chunk, merged)
    loads[1].wait()
    loads[2].wait()
    total_width = count * width
    tile = min(256, act.shape[-1])
    for chunk in chunks:
        forward(0, chunk)
    for chunk in chunks:
        arrive(0, chunk)
        centre = gathered[0, chunk, 0].astype(f32).sum(axis=-1, keepdims=True)
        for index in range(1, count):
            centre += gathered[0, chunk, index].astype(f32).sum(axis=-1, keepdims=True)
        centre = centre / total_width
        spread_sum = jnp.zeros_like(centre)
        for index in range(count):
            shifted = gathered[0, chunk, index].astype(f32) - centre
            spread_sum += (shifted * shifted).sum(axis=-1, keepdims=True)
        scale = lax.rsqrt(spread_sum / total_width + 1e-05)
        for index in range(count):
            shifted = gathered[0, chunk, index].astype(f32) - centre
            normed[chunk, :, index * width : (index + 1) * width] = (shifted * scale).astype(
                low_type
            )

        def hidden(index, carry):
            cut = pl.ds(pl.multiple_of(index * tile, tile), tile)
            values = jnp.dot(normed[chunk], w_in[:, cut], preferred_element_type=f32)
            act[chunk, :, cut] = jax.nn.gelu(values).astype(low_type)
            return carry

        lax.fori_loop(0, act.shape[-1] // tile, hidden, 0)
        start_y(1, chunk, act.at[chunk], w_out)
    for chunk in chunks:
        hold(chunk, act.at[chunk], w_out)
        start_z(1, chunk)
    for chunk in chunks:
        spread(1, chunk, own[chunk] + finish(1, chunk))
    for chunk in chunks:
        forward(1, chunk)
    loads[3].wait()
    for chunk in chunks:
        arrive(1, chunk)
        for index in range(count):
            normed[chunk, :, index * width : (index + 1) * width] = gathered[1, chunk, index]
        cols[...] = jnp.dot(normed[chunk], split[...], preferred_element_type=f32)
        for index in range(chips):
            values = cols[index * own_count : (index + 1) * own_count]
            sent3[chunk, index] = values.astype(low_type)
        for step in range(chips):
            peer = level(step) * 2 + chunk
            pl.when(peer != me)(lambda: last_copy(peer, me).start())
    pieces_ref[me] = sent3[y, z]
    for step in range(1, count):
        source = lax.rem(me + step, count)
        last_copy(source, source).wait_recv()
    for step in range(1, count):
        peer = lax.rem(me + step, count)
        first_copy(peer, me).wait_send()
        last_copy(peer, me).wait_send()
    for phase in (0, 1):
        for chunk in chunks:
            for step in range(chips):
                y_copy(phase, chunk, level(step)).wait_send()
                o_copy(phase, chunk, level(step), y).wait_send()
                if step > 0:
                    z_copy(phase, chunk, level(step), z).wait_send()
                    g_copy(phase, chunk, level(step), z).wait_send()


def coarse_scratch(count, own_count, depth, merge_two, mlp_in, mlp_out, split_weight):
    low, f32 = jnp.bfloat16, jnp.float32
    chips = count // 2
    tokens, top = chips * own_count, merge_two.shape[1]
    width, hidden, split_width = top // count, mlp_in.shape[1], split_weight.shape[1]
    dma = pltpu.SemaphoreType.DMA
    return [
        pltpu.VMEM(merge_two.shape, low),
        pltpu.VMEM(mlp_in.shape, low),
        pltpu.VMEM(mlp_out.shape, low),
        pltpu.VMEM(split_weight.shape, low),
        pltpu.VMEM((2, chips, own_count, depth), low),
        pltpu.VMEM((tokens, depth), f32),
        pltpu.VMEM((2, tokens, depth), low),
        pltpu.VMEM((2, 2, chips, tokens, width), low),
        pltpu.VMEM((2, 2, chips, tokens, width), low),
        pltpu.VMEM((2, 2, chips, tokens, width), low),
        pltpu.VMEM((2, 2, chips, tokens, width), low),
        pltpu.VMEM((2, chips, tokens, width), f32),
        pltpu.VMEM((2, tokens, width), f32),
        pltpu.VMEM((2, 2, count, tokens, width), low),
        pltpu.VMEM((2, tokens, top), low),
        pltpu.VMEM((2, tokens, hidden), low),
        pltpu.VMEM((tokens, split_width), f32),
        pltpu.VMEM((2, chips, own_count, split_width), low),
        dma((4,)),
        dma((count,)),
        dma((count,)),
    ] + [dma((2, 2, chips)) for _ in range(8)] + [dma((count,)), dma((count,))]


def coarse_kernel(*refs):
    count = lax.axis_size("lon")
    me = lax.axis_index("lon")

    def greet():
        barrier = pltpu.get_barrier_semaphore()
        for step in range(1, count):
            peer = lax.rem(me + step, count)
            pl.semaphore_signal(
                barrier, inc=1, device_id={"lon": peer}, device_id_type=pl.DeviceIdType.MESH
            )
        pl.semaphore_wait(barrier, count - 1)

    coarse_steps(*refs, greet)


def coarse_in_one(blocks, merge_two, mlp_in, mlp_out, split_weight):
    count, own_count, depth = blocks.shape
    whole = pl.BlockSpec(memory_space=pltpu.VMEM)
    apart = pl.BlockSpec(memory_space=pl.ANY)
    return pl.pallas_call(
        coarse_kernel,
        out_shape=jax.ShapeDtypeStruct((count, own_count, split_weight.shape[1]), jnp.bfloat16),
        in_specs=[whole, apart, apart, apart, apart],
        out_specs=whole,
        scratch_shapes=coarse_scratch(
            count, own_count, depth, merge_two, mlp_in, mlp_out, split_weight
        ),
        compiler_params=pltpu.CompilerParams(
            collective_id=0, has_side_effects=True, vmem_limit_bytes=60 * 1024 * 1024
        ),
    )(blocks, merge_two, mlp_in, mlp_out, split_weight)


def coarse_apart(normed2, merge_two, mlp_in, mlp_out, split_weight):
    own_count = normed2.shape[0]
    feature_parts = lax.all_to_all(normed2, "lon", split_axis=1, concat_axis=0, tiled=True)
    partial_value = jnp.dot(feature_parts, merge_two, preferred_element_type=jnp.float32)
    merged2 = lax.psum(partial_value.astype(jnp.bfloat16), "lon").astype(jnp.float32)
    normed3 = layer_norm(merged2).astype(jnp.bfloat16)
    act = jax.nn.gelu(jnp.dot(normed3, mlp_in, preferred_element_type=jnp.float32)).astype(
        jnp.bfloat16
    )
    mlp_own = lax.psum_scatter(
        jnp.dot(act, mlp_out, preferred_element_type=jnp.float32).astype(jnp.bfloat16),
        "lon",
        scatter_dimension=0,
        tiled=True,
    ).astype(jnp.float32)
    own_merged = lax.dynamic_slice_in_dim(merged2, lax.axis_index("lon") * own_count, own_count, 0)
    coarse = (own_merged + mlp_own).astype(jnp.bfloat16)
    split_cols = jnp.dot(
        lax.all_gather(coarse, "lon", axis=0, tiled=True),
        split_weight,
        preferred_element_type=jnp.float32,
    ).astype(jnp.bfloat16)
    return lax.all_to_all(split_cols, "lon", split_axis=0, concat_axis=1, tiled=True)


def halo_kernel(direction, shards, *refs):
    edges, weights = refs[:3], refs[3 : 3 + shards]
    came, wholes = refs[3 + shards : 6 + shards], refs[6 + shards : 6 + 2 * shards]
    edge_send, edge_recv, own_sem, weight_send, weight_recv = refs[6 + 2 * shards :]
    lat_count, lon_count = lax.axis_size("lat"), lax.axis_size("lon")
    row, col = lax.axis_index("lat"), lax.axis_index("lon")
    mesh = pl.DeviceIdType.MESH

    def beside(sign):
        next_row = lax.rem(row + sign + lat_count, lat_count)
        next_col = lax.rem(col + sign + lon_count, lon_count)
        return (next_row, col), (row, next_col), (next_row, next_col)

    other_core = row + 1 - 2 * lax.rem(row, 2)
    other_chip = lax.rem(row + 2, 4)
    side = lax.rem(col, 2)
    pair = col + 1 - 2 * side
    partners = beside(1) + beside(-1)
    if shards:
        partners += ((other_core, col), (other_chip, col), (row, pair))
    barrier = pltpu.get_barrier_semaphore()
    for partner in partners:
        pl.semaphore_signal(barrier, inc=1, device_id=partner, device_id_type=mesh)
    pl.semaphore_wait(barrier, len(partners))

    copies = []
    for index, target in enumerate(beside(direction)):
        copies.append(
            pltpu.make_async_remote_copy(
                src_ref=edges[index],
                dst_ref=came[index],
                send_sem=edge_send.at[index],
                recv_sem=edge_recv.at[index],
                device_id=target,
                device_id_type=mesh,
            )
        )
    for copy in copies:
        copy.start()

    def columns(index, owner):
        width = weights[index].shape[1]
        return wholes[index].at[:, pl.ds(pl.multiple_of(owner * width, width), width)]

    def half(ref, index, which):
        depth = weights[index].shape[0] // 2
        return ref.at[pl.ds(pl.multiple_of(which * depth, depth), depth)]

    def send(index, kind, source, target, device):
        copy = pltpu.make_async_remote_copy(
            src_ref=source,
            dst_ref=target,
            send_sem=weight_send.at[index, kind],
            recv_sem=weight_recv.at[index, kind],
            device_id=device,
            device_id_type=mesh,
        )
        copy.start()
        return copy

    moves = []
    for index in range(shards):
        mine, held = weights[index], columns(index, row)
        away = send(
            index, 0, half(mine, index, side), half(held, index, side), (other_chip, col)
        )
        moves.append([away, send(index, 1, mine, held, (other_core, col))])
        pltpu.make_async_copy(mine, held, own_sem.at[index]).start()
    for index in range(shards):
        moves[index][0].wait_recv()
        part = half(columns(index, other_chip), index, side)
        moves[index].append(send(index, 2, part, part, (row, pair)))
        moves[index].append(send(index, 3, part, part, (other_core, col)))
    for index in range(shards):
        moves[index][2].wait_recv()
        part = half(columns(index, other_chip), index, 1 - side)
        moves[index].append(send(index, 4, part, part, (other_core, col)))
    for index in range(shards):
        away, core, paired, first, second = moves[index]
        for copy in (away, core, paired, first, second):
            copy.wait_send()
        for copy in (core, first, second):
            copy.wait_recv()
        pltpu.make_async_copy(weights[index], columns(index, row), own_sem.at[index]).wait()
    for copy in copies:
        copy.wait()


def exchange(edges, direction, weights, identity):
    whole = pl.BlockSpec(memory_space=pltpu.VMEM)
    shards = len(weights)
    outs = [jax.ShapeDtypeStruct(edge.shape, edge.dtype) for edge in edges]
    outs += [
        jax.ShapeDtypeStruct((part.shape[0], 4 * part.shape[1]), part.dtype) for part in weights
    ]
    return pl.pallas_call(
        functools.partial(halo_kernel, direction, shards),
        out_shape=outs,
        in_specs=[whole] * (3 + shards),
        out_specs=[whole] * (3 + shards),
        scratch_shapes=[
            pltpu.SemaphoreType.DMA((3,)),
            pltpu.SemaphoreType.DMA((3,)),
            pltpu.SemaphoreType.DMA((max(shards, 1),)),
            pltpu.SemaphoreType.DMA((max(shards, 1), 5)),
            pltpu.SemaphoreType.DMA((max(shards, 1), 5)),
        ],
        compiler_params=pltpu.CompilerParams(collective_id=identity, has_side_effects=True),
    )(*edges, *weights)


def lat_swap(value, mask):
    return lax.ppermute(value, "lat", [(index, index ^ mask) for index in range(4)])


def in_owner_order(parts):
    index = lax.axis_index("lat")
    odd, high = index % 2 == 1, index >= 2
    a, b, c, d = parts
    a, b = jnp.where(odd, b, a), jnp.where(odd, a, b)
    c, d = jnp.where(odd, d, c), jnp.where(odd, c, d)
    a, c = jnp.where(high, c, a), jnp.where(high, a, c)
    b, d = jnp.where(high, d, b), jnp.where(high, b, d)
    return jnp.concatenate((a, b, c, d), axis=-1)


def attend_kernel(
    tok, qkv_hbm, proj_hbm, merge_hbm, fine_ref, merged_ref, blocks_ref,
    wq, wp, wm, low, came_row, came_low, packed, normed, qkv, bias, heads, low_back, row_back,
    attn, back_row, back_low, split_fine, cat, cat_low, parts, split_mid, cat2,
    halo_send, halo_recv, own_sem, weight_send, weight_recv,
):
    lat_count, lon_count = lax.axis_size("lat"), lax.axis_size("lon")
    row, col = lax.axis_index("lat"), lax.axis_index("lon")
    mesh = pl.DeviceIdType.MESH
    f32, low_type = jnp.float32, jnp.bfloat16
    rows, slots, width = tok.shape
    levels = 2
    near = levels * SHIFT_C
    edge = low.shape[1]
    head_dim = width // HEADS

    def beside(sign):
        next_row = lax.rem(row + sign + lat_count, lat_count)
        next_col = lax.rem(col + sign + lon_count, lon_count)
        return (next_row, col), (row, next_col), (next_row, next_col)

    other_core = row + 1 - 2 * lax.rem(row, 2)
    other_chip = lax.rem(row + 2, 4)
    far = lax.rem(other_core + 2, 4)
    side = lax.rem(col, 2)
    pair = col + 1 - 2 * side
    low[...] = tok[...].astype(f32)[:, :edge].astype(low_type)
    cat[...] = jnp.zeros_like(cat)
    partners = beside(1) + beside(-1) + ((other_core, col), (other_chip, col), (row, pair))
    barrier = pltpu.get_barrier_semaphore()
    for partner in partners:
        pl.semaphore_signal(barrier, inc=1, device_id=partner, device_id_type=mesh)
    pl.semaphore_wait(barrier, len(partners))

    shards = (qkv_hbm, proj_hbm, merge_hbm)
    counts = WEIGHT_PIECES

    def whole(index, owner):
        if index == 1:
            cut = proj_hbm.shape[1]
            return wp.at[:, pl.ds(pl.multiple_of(owner * cut, cut), cut)]
        return (wq if index == 0 else wm).at[owner]

    def piece(ref, index, which, number):
        depth = shards[index].shape[0] // 2
        size = depth // counts[index]
        start = pl.multiple_of(which * depth + number * size, size)
        return ref.at[pl.ds(start, size)]

    def send(index, kind, number, source, target, device):
        place = kind * max(counts) + number
        copy = pltpu.make_async_remote_copy(
            src_ref=source,
            dst_ref=target,
            send_sem=weight_send.at[index, place],
            recv_sem=weight_recv.at[index, place],
            device_id=device,
            device_id_type=mesh,
        )
        copy.start()
        return copy

    over, across, own = {}, {}, {}
    first, second, third = {}, {}, {}

    def send_over(index):
        for number in range(counts[index]):
            over[index, number] = send(
                index, 0, number,
                piece(shards[index], index, side, number),
                piece(whole(index, row), index, side, number),
                (other_chip, col),
            )

    def send_across(index):
        across[index] = send(
            index, 1, 0, shards[index], whole(index, row), (other_core, col)
        )
        own[index] = pltpu.make_async_copy(shards[index], whole(index, row), own_sem.at[index])
        own[index].start()

    def pass_on(index, number):
        over[index, number].wait_recv()
        held = piece(whole(index, other_chip), index, side, number)
        first[index, number] = send(index, 2, number, held, held, (row, pair))
        second[index, number] = send(index, 3, number, held, held, (other_core, col))

    def pass_last(index, number):
        first[index, number].wait_recv()
        held = piece(whole(index, other_chip), index, 1 - side, number)
        third[index, number] = send(index, 4, number, held, held, (other_core, col))

    def wait_far(index):
        for number in range(counts[index]):
            second[index, number].wait_recv()
            third[index, number].wait_recv()

    def halo(place, source, target, device):
        copy = pltpu.make_async_remote_copy(
            src_ref=source,
            dst_ref=target,
            send_sem=halo_send.at[place],
            recv_sem=halo_recv.at[place],
            device_id=device,
            device_id_type=mesh,
        )
        copy.start()
        return copy

    before, after = beside(-1), beside(1)
    there = [
        halo(0, low.at[SHIFT_R:], came_low.at[SHIFT_R:], before[1]),
        halo(1, low.at[:SHIFT_R], came_low.at[:SHIFT_R], before[2]),
    ]
    send_over(0)
    there.append(halo(2, tok.at[:SHIFT_R], came_row, before[0]))
    send_across(0)
    send_over(1)
    send_across(1)
    send_over(2)
    send_across(2)

    slot = lax.broadcasted_iota(jnp.int32, (1, edge, width), 1)
    tokens = WIN_R * slots
    wins = rows // WIN_R
    key_row = lax.broadcasted_iota(jnp.int32, (tokens, tokens), 1) >= (WIN_R - SHIFT_R) * slots
    query_row = lax.broadcasted_iota(jnp.int32, (tokens, tokens), 0) >= (WIN_R - SHIFT_R) * slots
    last = jnp.where(row == lat_count - 1, f32(-1000000000.0), f32(0.0))
    bias[...] = jnp.where(key_row == query_row, f32(0.0), last)

    for number in range(counts[0]):
        pass_on(0, number)
    for copy in there:
        copy.wait_recv()
    packed[: rows - SHIFT_R] = tok[SHIFT_R:].astype(f32)
    packed[rows - SHIFT_R :] = came_row[...].astype(f32)
    packed[: rows - SHIFT_R, :edge] = jnp.where(
        slot < near, came_low[SHIFT_R:].astype(f32), packed[: rows - SHIFT_R, :edge]
    )
    packed[rows - SHIFT_R :, :edge] = jnp.where(
        slot < near, came_low[:SHIFT_R].astype(f32), packed[rows - SHIFT_R :, :edge]
    )
    for win in range(wins):
        values = packed[win * WIN_R : (win + 1) * WIN_R].reshape(tokens, width)
        normed[win * tokens : (win + 1) * tokens] = layer_norm(values).astype(low_type)

    cut = qkv_hbm.shape[1]

    def project(owner):
        place = pl.ds(pl.multiple_of(owner * cut, cut), cut)
        qkv[:, place] = jnp.dot(
            normed[...], wq[owner], preferred_element_type=f32
        ).astype(low_type)

    own[0].wait()
    project(row)
    across[0].wait_recv()
    project(other_core)
    for number in range(counts[0]):
        pass_last(0, number)
    project(other_chip)
    wait_far(0)
    project(far)

    for number in range(counts[1]):
        pass_on(1, number)
    pass_on(2, 0)

    lane = lax.broadcasted_iota(jnp.int32, (1, 2 * head_dim), 1)
    near_head = jnp.where(lane < head_dim, 1.0, 0.0).astype(low_type)
    scale = 1.0 / math.sqrt(head_dim)

    def attend(win):
        place = pl.ds(win * tokens, tokens)

        def head_pair(index, carry):
            def columns(kind):
                start = pl.multiple_of(kind * width + index * 2 * head_dim, 2 * head_dim)
                return qkv[place, pl.ds(start, 2 * head_dim)]

            query, key, value = columns(0), columns(1), columns(2)
            outs = []
            for mask in (near_head, 1 - near_head):
                scores = lax.dot_general(
                    query, key * mask, (((1,), (1,)), ((), ())), preferred_element_type=f32
                )
                scores = scores * scale
                if win == wins - 1:
                    scores = scores + bias[...]
                expo = jnp.exp(scores - jnp.max(scores, axis=-1, keepdims=True))
                total = jnp.sum(expo, axis=-1, keepdims=True)
                out = jnp.dot(expo.astype(low_type), value, preferred_element_type=f32)
                outs.append(out / total)
            start = pl.multiple_of(index * 2 * head_dim, 2 * head_dim)
            heads[place, pl.ds(start, 2 * head_dim)] = jnp.where(
                lane < head_dim, outs[0], outs[1]
            ).astype(low_type)
            return carry

        lax.fori_loop(0, HEADS // 2, head_pair, 0)

    for win in range(wins):
        attend(win)
        if win == 0:
            for number in range(counts[1]):
                pass_last(1, number)
        pass_on(2, win + 1)
        pass_last(2, win)

    own[1].wait()
    across[1].wait_recv()
    wait_far(1)
    for win in range(wins):
        values = jnp.dot(
            heads[win * tokens : (win + 1) * tokens], wp[...], preferred_element_type=f32
        )
        values = values.astype(low_type).astype(f32).reshape(WIN_R, slots, width)
        attn[win * WIN_R : (win + 1) * WIN_R] = values
    low_back[...] = attn[:, :edge].astype(low_type)
    row_back[...] = attn[rows - SHIFT_R :].astype(low_type)
    kept = rows - SHIFT_R
    back = [
        halo(3, low_back.at[:kept], back_low.at[SHIFT_R:], after[1]),
        halo(4, low_back.at[kept:], back_low.at[:SHIFT_R], after[2]),
        halo(5, row_back, back_row, after[0]),
    ]
    for number in range(wins + 1, counts[2]):
        pass_on(2, number)
    for copy in back:
        copy.wait_recv()

    fine_ref[SHIFT_R:] = tok[SHIFT_R:].astype(f32) + attn[:kept]
    fine_ref[:SHIFT_R] = tok[:SHIFT_R].astype(f32) + back_row[...].astype(f32)
    fine_ref[:, :edge] = jnp.where(
        slot < near,
        tok[...].astype(f32)[:, :edge] + back_low[...].astype(f32),
        fine_ref[:, :edge],
    )

    group = cat.shape[0] // rows
    half_cols = slots // levels // 2
    lanes = 128
    for tile in range(width // lanes):
        split_fine[tile] = fine_ref[:, :, tile * lanes : (tile + 1) * lanes]
    for line in range(rows // 2):
        for level in range(levels):
            for part in range(4):
                start = levels * (part % 2) + level
                base = (line * levels + level) * group
                for tile in range(width // lanes):
                    place = part * width + tile * lanes
                    cat[base : base + half_cols, place : place + lanes] = split_fine[
                        tile, 2 * line + part // 2, pl.ds(start, half_cols, stride=2 * levels), :
                    ]
    for number in range(wins, counts[2]):
        pass_last(2, number)
    cat_low[...] = layer_norm(cat[...]).astype(low_type)
    wide = merge_hbm.shape[1]

    def merge(owner):
        values = jnp.dot(cat_low[...], wm[owner], preferred_element_type=f32)
        place = pl.ds(pl.multiple_of(owner * wide, wide), wide)
        parts[:, place] = values.astype(low_type).astype(f32)

    own[2].wait()
    merge(row)
    across[2].wait_recv()
    merge(other_core)
    merge(other_chip)
    wait_far(2)
    merge(far)
    merged_ref[...] = parts[...].astype(low_type)
    mid = parts.shape[1]
    for tile in range(mid // lanes):
        split_mid[tile] = parts[:, tile * lanes : (tile + 1) * lanes]
    quarter = half_cols // 2
    for line in range(rows // 4):
        for level in range(levels):
            for part in range(4):
                source = ((2 * line + part // 2) * levels + level) * group
                base = (line * levels + level) * quarter
                for tile in range(mid // lanes):
                    place = part * mid + tile * lanes
                    cat2[base : base + quarter, place : place + lanes] = split_mid[
                        tile, pl.ds(source + part % 2, quarter, stride=2), :
                    ]
    values = layer_norm(cat2[...]).astype(low_type)
    count, own_count, depth = blocks_ref.shape
    for index in range(count):
        blocks_ref[index] = values[:, index * depth : (index + 1) * depth]

    for copy in there + back:
        copy.wait_send()
    for copies in (over, across, first, second, third):
        for copy in copies.values():
            copy.wait_send()


WEIGHT_PIECES = (2, 1, 4)


def attend(tokens, qkv_weight, proj_weight, merge_one):
    rows, slots, width = tokens.shape
    low, f32 = jnp.bfloat16, jnp.float32
    levels = slots // (slots // 2)
    count = lax.axis_size("lon")
    near = levels * SHIFT_C
    edge = -(-near // 8) * 8
    half_cols = slots // levels // 2
    group = -(-half_cols // 8) * 8
    cats = rows // 2 * levels * group
    mid = 4 * merge_one.shape[1]
    own_count = rows // 4 * levels * (half_cols // 2)
    whole = pl.BlockSpec(memory_space=pltpu.VMEM)
    apart = pl.BlockSpec(memory_space=pl.ANY)
    tall = rows * slots
    return pl.pallas_call(
        attend_kernel,
        out_shape=[
            jax.ShapeDtypeStruct((rows, slots, width), f32),
            jax.ShapeDtypeStruct((cats, mid), low),
            jax.ShapeDtypeStruct((count, own_count, 4 * mid // count), low),
        ],
        in_specs=[whole, apart, apart, apart],
        out_specs=[whole] * 3,
        scratch_shapes=[
            pltpu.VMEM((4,) + qkv_weight.shape, low),
            pltpu.VMEM((proj_weight.shape[0], 4 * proj_weight.shape[1]), low),
            pltpu.VMEM((4,) + merge_one.shape, low),
            pltpu.VMEM((rows, edge, width), low),
            pltpu.VMEM((SHIFT_R, slots, width), low),
            pltpu.VMEM((rows, edge, width), low),
            pltpu.VMEM((rows, slots, width), f32),
            pltpu.VMEM((tall, width), low),
            pltpu.VMEM((tall, 3 * width), low),
            pltpu.VMEM((WIN_R * slots, WIN_R * slots), f32),
            pltpu.VMEM((tall, width), low),
            pltpu.VMEM((rows, edge, width), low),
            pltpu.VMEM((SHIFT_R, slots, width), low),
            pltpu.VMEM((rows, slots, width), f32),
            pltpu.VMEM((SHIFT_R, slots, width), low),
            pltpu.VMEM((rows, edge, width), low),
            pltpu.VMEM((width // 128, rows, slots, 128), f32),
            pltpu.VMEM((cats, 4 * width), f32),
            pltpu.VMEM((cats, 4 * width), low),
            pltpu.VMEM((cats, mid), f32),
            pltpu.VMEM((mid // 128, cats, 128), f32),
            pltpu.VMEM((own_count, 4 * mid), f32),
            pltpu.SemaphoreType.DMA((6,)),
            pltpu.SemaphoreType.DMA((6,)),
            pltpu.SemaphoreType.DMA((3,)),
            pltpu.SemaphoreType.DMA((3, 5 * max(WEIGHT_PIECES))),
            pltpu.SemaphoreType.DMA((3, 5 * max(WEIGHT_PIECES))),
        ],
        compiler_params=pltpu.CompilerParams(
            collective_id=3, has_side_effects=True, vmem_limit_bytes=60 * 1024 * 1024
        ),
    )(tokens, qkv_weight, proj_weight, merge_one)


def on_any(
    fine_tokens, qkv_weight, proj_weight, merge_one, merge_two, mlp_in, mlp_out, split_weight
):
    levels, rows, cols, width = fine_tokens.shape
    lat_count = lax.axis_size("lat")
    head_dim = width // HEADS
    edges = (
        fine_tokens[:, :SHIFT_R, SHIFT_C:],
        fine_tokens[:, SHIFT_R:, :SHIFT_C],
        fine_tokens[:, :SHIFT_R, :SHIFT_C],
    )
    if lat_count == 4 and lax.axis_size("lon") % 2 == 0:
        row_came, col_came, both_came, full_qkv, full_proj = exchange(
            edges, -1, (qkv_weight, proj_weight), 1
        )
        merge_one, row_came = lax.optimization_barrier((merge_one, row_came))
        merge_far = lat_swap(merge_one, 2)
        merge_parts = (merge_one, lat_swap(merge_one, 1), merge_far, lat_swap(merge_far, 1))
    else:
        row_came, col_came, both_came = exchange(edges, -1, (), 1)
        full_qkv = lax.all_gather(qkv_weight, "lat", axis=1, tiled=True)
        full_proj = lax.all_gather(proj_weight, "lat", axis=1, tiled=True)
    upper = jnp.concatenate([fine_tokens[:, SHIFT_R:, SHIFT_C:], col_came], axis=2)
    lower = jnp.concatenate([row_came, both_came], axis=2)
    moved = jnp.concatenate([upper, lower], axis=1)
    normed = layer_norm(moved.astype(jnp.float32)).astype(jnp.bfloat16).reshape(-1, width)
    qkv = jnp.dot(normed, full_qkv, preferred_element_type=jnp.float32).astype(jnp.bfloat16)
    row_wins = rows // WIN_R
    col_wins = cols // WIN_C
    wins = row_wins * col_wins
    tokens = levels * WIN_R * WIN_C
    parts = qkv.reshape(levels, row_wins, WIN_R, col_wins, WIN_C, 3, HEADS, head_dim)
    parts = parts.transpose(1, 3, 0, 2, 4, 5, 6, 7).reshape(wins, tokens, 3, HEADS, head_dim)
    scores = jnp.einsum(
        "wqhd,wkhd->whqk", parts[:, :, 0], parts[:, :, 1], preferred_element_type=jnp.float32
    )
    scores = scores / math.sqrt(head_dim)
    global_rows = lax.axis_index("lat") * rows + jnp.arange(rows, dtype=jnp.int32)
    wrapped = (global_rows >= rows * lat_count - SHIFT_R).astype(jnp.int32).reshape(row_wins, WIN_R)
    labels = jnp.broadcast_to(
        wrapped[:, None, None, :, None], (row_wins, col_wins, levels, WIN_R, WIN_C)
    )
    labels = labels.reshape(wins, tokens)
    allowed = labels[:, :, None] == labels[:, None, :]
    scores = jnp.where(allowed[:, None], scores, jnp.float32(-1000000000.0))
    top = jnp.max(scores, axis=-1, keepdims=True)
    expo = jnp.exp(scores - top)
    probs = (expo / jnp.sum(expo, axis=-1, keepdims=True)).astype(jnp.bfloat16)
    heads_out = jnp.einsum(
        "whqk,wkhd->wqhd", probs, parts[:, :, 2], preferred_element_type=jnp.float32
    )
    heads_out = heads_out.astype(jnp.bfloat16).reshape(
        row_wins, col_wins, levels, WIN_R, WIN_C, width
    )
    heads_out = heads_out.transpose(2, 0, 3, 1, 4, 5).reshape(-1, width)
    attn = jnp.dot(heads_out, full_proj, preferred_element_type=jnp.float32).astype(jnp.bfloat16)
    attn = attn.reshape(levels, rows, cols, width)
    edges = (
        attn[:, rows - SHIFT_R :, : cols - SHIFT_C],
        attn[:, : rows - SHIFT_R, cols - SHIFT_C :],
        attn[:, rows - SHIFT_R :, cols - SHIFT_C :],
    )
    row_came, col_came, both_came = exchange(edges, 1, (), 2)
    upper = jnp.concatenate([both_came, row_came], axis=2)
    lower = jnp.concatenate([col_came, attn[:, : rows - SHIFT_R, : cols - SHIFT_C]], axis=2)
    back = jnp.concatenate([upper, lower], axis=1)
    fine_out = fine_tokens.astype(jnp.float32) + back.astype(jnp.float32)
    normed1 = layer_norm(cat_four(fine_out)).astype(jnp.bfloat16)
    if lat_count == 4 and lax.axis_size("lon") % 2 == 0:
        merged1 = in_owner_order(
            [
                jnp.dot(normed1, part, preferred_element_type=jnp.float32).astype(jnp.bfloat16)
                for part in merge_parts
            ]
        )
    else:
        merge_all = lax.all_gather(merge_one, "lat", axis=1, tiled=True)
        merged1 = jnp.dot(normed1, merge_all, preferred_element_type=jnp.float32)
        merged1 = merged1.astype(jnp.bfloat16)
    merged1 = merged1.reshape(levels, rows // 2, cols // 2, MID)
    normed2 = layer_norm(cat_four(merged1.astype(jnp.float32))).astype(jnp.bfloat16)
    count = lax.axis_size("lon")
    if count % 2 == 0 and merge_two.shape[1] % (count * 128) == 0:
        blocks = normed2.reshape(normed2.shape[0], count, -1).transpose(1, 0, 2)
        pieces = coarse_in_one(blocks, merge_two, mlp_in, mlp_out, split_weight)
        pieces = pieces.transpose(1, 0, 2)
    else:
        pieces = coarse_apart(normed2, merge_two, mlp_in, mlp_out, split_weight)
    pieces = pieces.reshape(levels, rows // 4, cols // 4, 2, 2, MID).transpose(0, 1, 3, 2, 4, 5)
    pieces = pieces.reshape(levels, rows // 2, cols // 2, MID)
    mid_out = merged1.astype(jnp.float32) + pieces.astype(jnp.float32)
    return (fine_out, mid_out)


def on_device(
    fine_tokens, qkv_weight, proj_weight, merge_one, merge_two, mlp_in, mlp_out, split_weight
):
    levels, rows, cols, width = fine_tokens.shape
    lat_count, count = lax.axis_size("lat"), lax.axis_size("lon")
    fits = count % 2 == 0 and merge_two.shape[1] % (count * 128) == 0
    if lat_count != 4 or not fits or rows != 2 * WIN_R or cols != WIN_C or levels != 2:
        return on_any(
            fine_tokens, qkv_weight, proj_weight, merge_one, merge_two, mlp_in, mlp_out, split_weight
        )
    tokens = fine_tokens.transpose(1, 2, 0, 3).reshape(rows, cols * levels, width)
    fine, merged1, blocks = attend(tokens, qkv_weight, proj_weight, merge_one)
    fine_out = fine.reshape(rows, cols, levels, width).transpose(2, 0, 1, 3)
    pieces = coarse_in_one(blocks, merge_two, mlp_in, mlp_out, split_weight)
    half_rows, half_cols = rows // 2, cols // 2
    pieces = pieces.transpose(1, 0, 2).reshape(rows // 4, levels, cols // 4, 2, 2, MID)
    pieces = pieces.transpose(0, 3, 2, 4, 1, 5).reshape(half_rows, half_cols, levels, MID)
    merged1 = merged1.reshape(half_rows, levels, -1, MID)[:, :, :half_cols].transpose(0, 2, 1, 3)
    mid_out = merged1.astype(jnp.float32) + pieces.astype(jnp.float32)
    return (fine_out, mid_out.transpose(2, 0, 1, 3))


def solution(mesh):
    return jax.shard_map(
        on_device,
        mesh=mesh,
        in_specs=(
            P(None, "lat", "lon", None),
            P(None, "lat"),
            P(None, "lat"),
            P(None, "lat"),
            P("lon", None),
            P(None, "lon"),
            P("lon", None),
            P(None, "lon"),
        ),
        out_specs=(P(None, "lat", "lon", None), P(None, "lat", "lon", None)),
        check_vma=False,
    )
```

```python
import functools
import math

import jax
import jax.numpy as jnp
from jax import lax
from jax.experimental import pallas as pl
from jax.experimental.pallas import tpu as pltpu
from jax.sharding import PartitionSpec as P

MID = 1024
HEADS = 8
WIN_R = 6
WIN_C = 12
SHIFT_R = 3
SHIFT_C = 6


def layer_norm(values):
    centre = jnp.mean(values, axis=-1, keepdims=True)
    shifted = values - centre
    spread = jnp.mean(shifted * shifted, axis=-1, keepdims=True)
    return shifted * lax.rsqrt(spread + 1e-05)


def cat_four(grid):
    lev, rows, cols, width = grid.shape
    grid = grid.reshape(lev, rows // 2, 2, cols // 2, 2, width).transpose(0, 1, 3, 2, 4, 5)
    return grid.reshape(lev * (rows // 2) * (cols // 2), 4 * width)


def coarse_loads(sources, targets, sems):
    return [
        pltpu.make_async_copy(source, target, sems.at[index])
        for index, (source, target) in enumerate(zip(sources, targets))
    ]


def coarse_steps(
    blocks_ref, two_hbm, in_hbm, out_hbm, split_hbm, pieces_ref,
    two, w_in, w_out, split, landed, features, feat, y_sent, y_land, z_sent, z_land, held, own,
    gathered, normed, act, cols, sent3,
    load_sem, first_send, first_recv, y_send, y_recv, z_send, z_recv, g_send, g_recv, o_send,
    o_recv, last_send, last_recv,
):
    count = lax.axis_size("lon")
    me = lax.axis_index("lon")
    chips = count // 2
    z, y = me // 2, lax.rem(me, 2)
    partner = me + 1 - 2 * y
    own_count = blocks_ref.shape[1]
    width = own.shape[-1]
    low_type, f32 = jnp.bfloat16, jnp.float32
    loads = coarse_loads((two_hbm, in_hbm, out_hbm, split_hbm), (two, w_in, w_out, split), load_sem)
    far_first = list(range(2, chips)) + [1] if chips > 2 else list(range(1, chips))

    def level(step):
        return lax.rem(z + step, chips)

    def remote(source, target, sent, came, peer):
        return pltpu.make_async_remote_copy(
            src_ref=source,
            dst_ref=target,
            send_sem=sent,
            recv_sem=came,
            device_id={"lon": peer},
            device_id_type=pl.DeviceIdType.MESH,
        )

    def first_copy(peer, source):
        return remote(
            blocks_ref.at[peer],
            landed.at[lax.rem(source, 2), source // 2],
            first_send.at[peer],
            first_recv.at[source],
            peer,
        )

    def y_copy(phase, chunk, block):
        return remote(
            y_sent.at[phase, chunk, block],
            y_land.at[phase, chunk, block],
            y_send.at[phase, chunk, block],
            y_recv.at[phase, chunk, block],
            partner,
        )

    def z_copy(phase, chunk, to, source):
        return remote(
            z_sent.at[phase, chunk, to],
            z_land.at[phase, chunk, source],
            z_send.at[phase, chunk, to],
            z_recv.at[phase, chunk, source],
            to * 2 + y,
        )

    def g_copy(phase, chunk, to, source):
        place = gathered.at[phase, chunk, source * 2 + y]
        return remote(
            place, place, g_send.at[phase, chunk, to], g_recv.at[phase, chunk, source], to * 2 + y
        )

    def o_copy(phase, chunk, block, side):
        place = gathered.at[phase, chunk, block * 2 + side]
        return remote(
            place, place, o_send.at[phase, chunk, block], o_recv.at[phase, chunk, block], partner
        )

    def last_copy(peer, source):
        return remote(
            sent3.at[lax.rem(peer, 2), peer // 2],
            pieces_ref.at[source],
            last_send.at[peer],
            last_recv.at[source],
            peer,
        )

    def product(left, weight, peer):
        cut = pl.ds(pl.multiple_of(peer * width, width), width)
        return jnp.dot(left[...], weight[:, cut], preferred_element_type=f32)

    def start_y(phase, chunk, left, weight):
        for step in far_first + [0]:
            block = level(step)
            y_sent[phase, chunk, block] = product(left, weight, block * 2 + 1 - y).astype(low_type)
            y_copy(phase, chunk, block).start()

    def hold(chunk, left, weight):
        for step in far_first + [0]:
            block = level(step)
            held[chunk, block] = product(left, weight, block * 2 + y)

    def start_z(phase, chunk):
        for step in far_first:
            block = level(step)
            y_copy(phase, chunk, block).wait_recv()
            total = held[chunk, block] + y_land[phase, chunk, block].astype(f32)
            z_sent[phase, chunk, block] = total.astype(low_type)
            z_copy(phase, chunk, block, z).start()

    def finish(phase, chunk):
        y_copy(phase, chunk, z).wait_recv()
        total = held[chunk, z] + y_land[phase, chunk, z].astype(f32)
        for step in range(1, chips):
            block = level(step)
            z_copy(phase, chunk, block, block).wait_recv()
            total = total + z_land[phase, chunk, block].astype(f32)
        return total

    def spread(phase, chunk, values):
        gathered[phase, chunk, me] = values.astype(low_type)
        for step in far_first:
            g_copy(phase, chunk, level(step), z).start()
        o_copy(phase, chunk, z, y).start()

    def forward(phase, chunk):
        for step in range(1, chips):
            block = level(step)
            g_copy(phase, chunk, block, block).wait_recv()
            o_copy(phase, chunk, block, y).start()

    def arrive(phase, chunk):
        for step in range(chips):
            o_copy(phase, chunk, level(step), 1 - y).wait_recv()

    for step in range(1, count):
        first_copy(lax.rem(me + step, count), me).start()
    landed[y, z] = blocks_ref[me]
    chunks = (0, 1)
    for chunk in chunks:
        for index in range(chips):
            source = index * 2 + chunk
            pl.when(source != me)(lambda: first_copy(source, source).wait_recv())
        for index in range(chips):
            features[index * own_count : (index + 1) * own_count] = landed[chunk, index].astype(f32)
        feat[chunk] = features[...].astype(low_type)
        if chunk == 0:
            loads[0].wait()
        start_y(0, chunk, feat.at[chunk], two)
    for chunk in chunks:
        hold(chunk, feat.at[chunk], two)
        start_z(0, chunk)
    for chunk in chunks:
        merged = finish(0, chunk)
        own[chunk] = merged
        spread(0, chunk, merged)
    loads[1].wait()
    loads[2].wait()
    total_width = count * width
    tile = min(256, act.shape[-1])
    for chunk in chunks:
        forward(0, chunk)
    for chunk in chunks:
        arrive(0, chunk)
        centre = gathered[0, chunk, 0].astype(f32).sum(axis=-1, keepdims=True)
        for index in range(1, count):
            centre += gathered[0, chunk, index].astype(f32).sum(axis=-1, keepdims=True)
        centre = centre / total_width
        spread_sum = jnp.zeros_like(centre)
        for index in range(count):
            shifted = gathered[0, chunk, index].astype(f32) - centre
            spread_sum += (shifted * shifted).sum(axis=-1, keepdims=True)
        scale = lax.rsqrt(spread_sum / total_width + 1e-05)
        for index in range(count):
            shifted = gathered[0, chunk, index].astype(f32) - centre
            normed[chunk, :, index * width : (index + 1) * width] = (shifted * scale).astype(
                low_type
            )

        def hidden(index, carry):
            cut = pl.ds(pl.multiple_of(index * tile, tile), tile)
            values = jnp.dot(normed[chunk], w_in[:, cut], preferred_element_type=f32)
            act[chunk, :, cut] = jax.nn.gelu(values).astype(low_type)
            return carry

        lax.fori_loop(0, act.shape[-1] // tile, hidden, 0)
        start_y(1, chunk, act.at[chunk], w_out)
    for chunk in chunks:
        hold(chunk, act.at[chunk], w_out)
        start_z(1, chunk)
    for chunk in chunks:
        spread(1, chunk, own[chunk] + finish(1, chunk))
    for chunk in chunks:
        forward(1, chunk)
    loads[3].wait()
    for chunk in chunks:
        arrive(1, chunk)
        for index in range(count):
            normed[chunk, :, index * width : (index + 1) * width] = gathered[1, chunk, index]
        cols[...] = jnp.dot(normed[chunk], split[...], preferred_element_type=f32)
        for index in range(chips):
            values = cols[index * own_count : (index + 1) * own_count]
            sent3[chunk, index] = values.astype(low_type)
        for step in range(chips):
            peer = level(step) * 2 + chunk
            pl.when(peer != me)(lambda: last_copy(peer, me).start())
    pieces_ref[me] = sent3[y, z]
    for step in range(1, count):
        source = lax.rem(me + step, count)
        last_copy(source, source).wait_recv()
    for step in range(1, count):
        peer = lax.rem(me + step, count)
        first_copy(peer, me).wait_send()
        last_copy(peer, me).wait_send()
    for phase in (0, 1):
        for chunk in chunks:
            for step in range(chips):
                y_copy(phase, chunk, level(step)).wait_send()
                o_copy(phase, chunk, level(step), y).wait_send()
                if step > 0:
                    z_copy(phase, chunk, level(step), z).wait_send()
                    g_copy(phase, chunk, level(step), z).wait_send()


def coarse_scratch(count, own_count, depth, merge_two, mlp_in, mlp_out, split_weight):
    low, f32 = jnp.bfloat16, jnp.float32
    chips = count // 2
    tokens, top = chips * own_count, merge_two.shape[1]
    width, hidden, split_width = top // count, mlp_in.shape[1], split_weight.shape[1]
    dma = pltpu.SemaphoreType.DMA
    return [
        pltpu.VMEM(merge_two.shape, low),
        pltpu.VMEM(mlp_in.shape, low),
        pltpu.VMEM(mlp_out.shape, low),
        pltpu.VMEM(split_weight.shape, low),
        pltpu.VMEM((2, chips, own_count, depth), low),
        pltpu.VMEM((tokens, depth), f32),
        pltpu.VMEM((2, tokens, depth), low),
        pltpu.VMEM((2, 2, chips, tokens, width), low),
        pltpu.VMEM((2, 2, chips, tokens, width), low),
        pltpu.VMEM((2, 2, chips, tokens, width), low),
        pltpu.VMEM((2, 2, chips, tokens, width), low),
        pltpu.VMEM((2, chips, tokens, width), f32),
        pltpu.VMEM((2, tokens, width), f32),
        pltpu.VMEM((2, 2, count, tokens, width), low),
        pltpu.VMEM((2, tokens, top), low),
        pltpu.VMEM((2, tokens, hidden), low),
        pltpu.VMEM((tokens, split_width), f32),
        pltpu.VMEM((2, chips, own_count, split_width), low),
        dma((4,)),
        dma((count,)),
        dma((count,)),
    ] + [dma((2, 2, chips)) for _ in range(8)] + [dma((count,)), dma((count,))]


def coarse_apart(normed2, merge_two, mlp_in, mlp_out, split_weight):
    own_count = normed2.shape[0]
    feature_parts = lax.all_to_all(normed2, "lon", split_axis=1, concat_axis=0, tiled=True)
    partial_value = jnp.dot(feature_parts, merge_two, preferred_element_type=jnp.float32)
    merged2 = lax.psum(partial_value.astype(jnp.bfloat16), "lon").astype(jnp.float32)
    normed3 = layer_norm(merged2).astype(jnp.bfloat16)
    act = jax.nn.gelu(jnp.dot(normed3, mlp_in, preferred_element_type=jnp.float32)).astype(
        jnp.bfloat16
    )
    mlp_own = lax.psum_scatter(
        jnp.dot(act, mlp_out, preferred_element_type=jnp.float32).astype(jnp.bfloat16),
        "lon",
        scatter_dimension=0,
        tiled=True,
    ).astype(jnp.float32)
    own_merged = lax.dynamic_slice_in_dim(merged2, lax.axis_index("lon") * own_count, own_count, 0)
    coarse = (own_merged + mlp_own).astype(jnp.bfloat16)
    split_cols = jnp.dot(
        lax.all_gather(coarse, "lon", axis=0, tiled=True),
        split_weight,
        preferred_element_type=jnp.float32,
    ).astype(jnp.bfloat16)
    return lax.all_to_all(split_cols, "lon", split_axis=0, concat_axis=1, tiled=True)


def halo_kernel(direction, shards, *refs):
    edges, weights = refs[:3], refs[3 : 3 + shards]
    came, wholes = refs[3 + shards : 6 + shards], refs[6 + shards : 6 + 2 * shards]
    edge_send, edge_recv, own_sem, weight_send, weight_recv = refs[6 + 2 * shards :]
    lat_count, lon_count = lax.axis_size("lat"), lax.axis_size("lon")
    row, col = lax.axis_index("lat"), lax.axis_index("lon")
    mesh = pl.DeviceIdType.MESH

    def beside(sign):
        next_row = lax.rem(row + sign + lat_count, lat_count)
        next_col = lax.rem(col + sign + lon_count, lon_count)
        return (next_row, col), (row, next_col), (next_row, next_col)

    other_core = row + 1 - 2 * lax.rem(row, 2)
    other_chip = lax.rem(row + 2, 4)
    side = lax.rem(col, 2)
    pair = col + 1 - 2 * side
    partners = beside(1) + beside(-1)
    if shards:
        partners += ((other_core, col), (other_chip, col), (row, pair))
    barrier = pltpu.get_barrier_semaphore()
    for partner in partners:
        pl.semaphore_signal(barrier, inc=1, device_id=partner, device_id_type=mesh)
    pl.semaphore_wait(barrier, len(partners))

    copies = []
    for index, target in enumerate(beside(direction)):
        copies.append(
            pltpu.make_async_remote_copy(
                src_ref=edges[index],
                dst_ref=came[index],
                send_sem=edge_send.at[index],
                recv_sem=edge_recv.at[index],
                device_id=target,
                device_id_type=mesh,
            )
        )
    for copy in copies:
        copy.start()

    def columns(index, owner):
        width = weights[index].shape[1]
        return wholes[index].at[:, pl.ds(pl.multiple_of(owner * width, width), width)]

    def half(ref, index, which):
        depth = weights[index].shape[0] // 2
        return ref.at[pl.ds(pl.multiple_of(which * depth, depth), depth)]

    def send(index, kind, source, target, device):
        copy = pltpu.make_async_remote_copy(
            src_ref=source,
            dst_ref=target,
            send_sem=weight_send.at[index, kind],
            recv_sem=weight_recv.at[index, kind],
            device_id=device,
            device_id_type=mesh,
        )
        copy.start()
        return copy

    moves = []
    for index in range(shards):
        mine, held = weights[index], columns(index, row)
        away = send(
            index, 0, half(mine, index, side), half(held, index, side), (other_chip, col)
        )
        moves.append([away, send(index, 1, mine, held, (other_core, col))])
        pltpu.make_async_copy(mine, held, own_sem.at[index]).start()
    for index in range(shards):
        moves[index][0].wait_recv()
        part = half(columns(index, other_chip), index, side)
        moves[index].append(send(index, 2, part, part, (row, pair)))
        moves[index].append(send(index, 3, part, part, (other_core, col)))
    for index in range(shards):
        moves[index][2].wait_recv()
        part = half(columns(index, other_chip), index, 1 - side)
        moves[index].append(send(index, 4, part, part, (other_core, col)))
    for index in range(shards):
        away, core, paired, first, second = moves[index]
        for copy in (away, core, paired, first, second):
            copy.wait_send()
        for copy in (core, first, second):
            copy.wait_recv()
        pltpu.make_async_copy(weights[index], columns(index, row), own_sem.at[index]).wait()
    for copy in copies:
        copy.wait()


def exchange(edges, direction, weights, identity):
    whole = pl.BlockSpec(memory_space=pltpu.VMEM)
    shards = len(weights)
    outs = [jax.ShapeDtypeStruct(edge.shape, edge.dtype) for edge in edges]
    outs += [
        jax.ShapeDtypeStruct((part.shape[0], 4 * part.shape[1]), part.dtype) for part in weights
    ]
    return pl.pallas_call(
        functools.partial(halo_kernel, direction, shards),
        out_shape=outs,
        in_specs=[whole] * (3 + shards),
        out_specs=[whole] * (3 + shards),
        scratch_shapes=[
            pltpu.SemaphoreType.DMA((3,)),
            pltpu.SemaphoreType.DMA((3,)),
            pltpu.SemaphoreType.DMA((max(shards, 1),)),
            pltpu.SemaphoreType.DMA((max(shards, 1), 5)),
            pltpu.SemaphoreType.DMA((max(shards, 1), 5)),
        ],
        compiler_params=pltpu.CompilerParams(collective_id=identity, has_side_effects=True),
    )(*edges, *weights)


def lat_swap(value, mask):
    return lax.ppermute(value, "lat", [(index, index ^ mask) for index in range(4)])


def in_owner_order(parts):
    index = lax.axis_index("lat")
    odd, high = index % 2 == 1, index >= 2
    a, b, c, d = parts
    a, b = jnp.where(odd, b, a), jnp.where(odd, a, b)
    c, d = jnp.where(odd, d, c), jnp.where(odd, c, d)
    a, c = jnp.where(high, c, a), jnp.where(high, a, c)
    b, d = jnp.where(high, d, b), jnp.where(high, b, d)
    return jnp.concatenate((a, b, c, d), axis=-1)


def attend_kernel(
    tok, qkv_hbm, proj_hbm, merge_hbm, fine_ref, blocks_ref,
    wq, wp, wm, low, came_row, came_low, packed, normed, qkv, bias, heads, low_back, row_back,
    attn, back_row, back_low, split_fine, cat, cat_low, parts, split_mid, cat2,
    halo_send, halo_recv, own_sem, weight_send, weight_recv, start_loads,
):
    lat_count, lon_count = lax.axis_size("lat"), lax.axis_size("lon")
    row, col = lax.axis_index("lat"), lax.axis_index("lon")
    mesh = pl.DeviceIdType.MESH
    f32, low_type = jnp.float32, jnp.bfloat16
    rows, slots, width = tok.shape
    levels = 2
    near = levels * SHIFT_C
    edge = low.shape[1]
    head_dim = width // HEADS

    def beside(sign):
        next_row = lax.rem(row + sign + lat_count, lat_count)
        next_col = lax.rem(col + sign + lon_count, lon_count)
        return (next_row, col), (row, next_col), (next_row, next_col)

    other_core = row + 1 - 2 * lax.rem(row, 2)
    other_chip = lax.rem(row + 2, 4)
    far = lax.rem(other_core + 2, 4)
    side = lax.rem(col, 2)
    pair = col + 1 - 2 * side
    high_side = lax.rem(col // 2, 2)
    high_pair = col + 2 - 4 * high_side
    sides, pairs = (side, side, high_side), (pair, pair, high_pair)
    low[...] = tok[...].astype(f32)[:, :edge].astype(low_type)
    cat[...] = jnp.zeros_like(cat)
    partners = beside(1) + beside(-1) + ((other_core, col), (other_chip, col))
    partners += tuple((row, lax.rem(col + step, lon_count)) for step in range(1, lon_count))
    barrier = pltpu.get_barrier_semaphore()
    for partner in partners:
        pl.semaphore_signal(barrier, inc=1, device_id=partner, device_id_type=mesh)
    pl.semaphore_wait(barrier, len(partners))

    shards = (qkv_hbm, proj_hbm, merge_hbm)
    counts = WEIGHT_PIECES

    def whole(index, owner):
        if index == 1:
            cut = proj_hbm.shape[1]
            return wp.at[:, pl.ds(pl.multiple_of(owner * cut, cut), cut)]
        return (wq if index == 0 else wm).at[owner]

    def piece(ref, index, which, number):
        depth = shards[index].shape[0] // 2
        size = depth // counts[index]
        start = pl.multiple_of(which * depth + number * size, size)
        return ref.at[pl.ds(start, size)]

    def send(index, kind, number, source, target, device):
        place = kind * max(counts) + number
        copy = pltpu.make_async_remote_copy(
            src_ref=source,
            dst_ref=target,
            send_sem=weight_send.at[index, place],
            recv_sem=weight_recv.at[index, place],
            device_id=device,
            device_id_type=mesh,
        )
        copy.start()
        return copy

    over, across, own = {}, {}, {}
    first, second, third = {}, {}, {}

    def send_over(index):
        for number in range(counts[index]):
            over[index, number] = send(
                index, 0, number,
                piece(shards[index], index, sides[index], number),
                piece(whole(index, row), index, sides[index], number),
                (other_chip, col),
            )

    def send_across(index):
        across[index] = send(
            index, 1, 0, shards[index], whole(index, row), (other_core, col)
        )
        own[index] = pltpu.make_async_copy(shards[index], whole(index, row), own_sem.at[index])
        own[index].start()

    def pass_on(index, number):
        over[index, number].wait_recv()
        held = piece(whole(index, other_chip), index, sides[index], number)
        first[index, number] = send(index, 2, number, held, held, (row, pairs[index]))
        second[index, number] = send(index, 3, number, held, held, (other_core, col))

    def pass_last(index, number):
        first[index, number].wait_recv()
        held = piece(whole(index, other_chip), index, 1 - sides[index], number)
        third[index, number] = send(index, 4, number, held, held, (other_core, col))

    def wait_far(index):
        for number in range(counts[index]):
            second[index, number].wait_recv()
            third[index, number].wait_recv()

    def halo(place, source, target, device):
        copy = pltpu.make_async_remote_copy(
            src_ref=source,
            dst_ref=target,
            send_sem=halo_send.at[place],
            recv_sem=halo_recv.at[place],
            device_id=device,
            device_id_type=mesh,
        )
        copy.start()
        return copy

    before, after = beside(-1), beside(1)
    there = [
        halo(0, low.at[SHIFT_R:], came_low.at[SHIFT_R:], before[1]),
        halo(1, low.at[:SHIFT_R], came_low.at[:SHIFT_R], before[2]),
    ]
    there.append(halo(2, tok.at[:SHIFT_R], came_row, before[0]))
    send_over(0)
    send_across(0)
    send_over(1)
    send_across(1)
    send_over(2)
    send_across(2)
    start_loads()

    slot = lax.broadcasted_iota(jnp.int32, (1, edge, width), 1)
    tokens = WIN_R * slots
    wins = rows // WIN_R
    key_row = lax.broadcasted_iota(jnp.int32, (tokens, tokens), 1) >= (WIN_R - SHIFT_R) * slots
    query_row = lax.broadcasted_iota(jnp.int32, (tokens, tokens), 0) >= (WIN_R - SHIFT_R) * slots
    last = jnp.where(row == lat_count - 1, f32(-1000000000.0), f32(0.0))
    bias[...] = jnp.where(key_row == query_row, f32(0.0), last)

    for number in range(counts[0]):
        pass_on(0, number)
    for copy in there:
        copy.wait_recv()
    packed[: rows - SHIFT_R] = tok[SHIFT_R:].astype(f32)
    packed[rows - SHIFT_R :] = came_row[...].astype(f32)
    packed[: rows - SHIFT_R, :edge] = jnp.where(
        slot < near, came_low[SHIFT_R:].astype(f32), packed[: rows - SHIFT_R, :edge]
    )
    packed[rows - SHIFT_R :, :edge] = jnp.where(
        slot < near, came_low[:SHIFT_R].astype(f32), packed[rows - SHIFT_R :, :edge]
    )
    for win in range(wins):
        values = packed[win * WIN_R : (win + 1) * WIN_R].reshape(tokens, width)
        normed[win * tokens : (win + 1) * tokens] = layer_norm(values).astype(low_type)

    cut = qkv_hbm.shape[1]

    def project(owner):
        place = pl.ds(pl.multiple_of(owner * cut, cut), cut)
        qkv[:, place] = jnp.dot(
            normed[...], wq[owner], preferred_element_type=f32
        ).astype(low_type)

    own[0].wait()
    project(row)
    across[0].wait_recv()
    project(other_core)
    for number in range(counts[0]):
        pass_last(0, number)
    project(other_chip)
    wait_far(0)
    project(far)

    for number in range(counts[1]):
        pass_on(1, number)
    pass_on(2, 0)

    lane = lax.broadcasted_iota(jnp.int32, (1, 2 * head_dim), 1)
    near_head = jnp.where(lane < head_dim, 1.0, 0.0).astype(low_type)
    scale = 1.0 / math.sqrt(head_dim)

    def attend(win):
        place = pl.ds(win * tokens, tokens)

        def head_pair(index, carry):
            def columns(kind):
                start = pl.multiple_of(kind * width + index * 2 * head_dim, 2 * head_dim)
                return qkv[place, pl.ds(start, 2 * head_dim)]

            query, key, value = columns(0), columns(1), columns(2)
            outs = []
            for mask in (near_head, 1 - near_head):
                scores = lax.dot_general(
                    query, key * mask, (((1,), (1,)), ((), ())), preferred_element_type=f32
                )
                scores = scores * scale
                if win == wins - 1:
                    scores = scores + bias[...]
                expo = jnp.exp(scores - jnp.max(scores, axis=-1, keepdims=True))
                total = jnp.sum(expo, axis=-1, keepdims=True)
                out = jnp.dot(expo.astype(low_type), value, preferred_element_type=f32)
                outs.append(out / total)
            start = pl.multiple_of(index * 2 * head_dim, 2 * head_dim)
            heads[place, pl.ds(start, 2 * head_dim)] = jnp.where(
                lane < head_dim, outs[0], outs[1]
            ).astype(low_type)
            return carry

        lax.fori_loop(0, HEADS // 2, head_pair, 0)

    for win in range(wins):
        attend(win)
        if win == 0:
            pass_on(2, 1)

    for number in range(counts[1]):
        pass_last(1, number)
    own[1].wait()
    across[1].wait_recv()
    wait_far(1)
    for win in range(wins):
        values = jnp.dot(
            heads[win * tokens : (win + 1) * tokens], wp[...], preferred_element_type=f32
        )
        values = values.astype(low_type).astype(f32).reshape(WIN_R, slots, width)
        attn[win * WIN_R : (win + 1) * WIN_R] = values
    low_back[...] = attn[:, :edge].astype(low_type)
    row_back[...] = attn[rows - SHIFT_R :].astype(low_type)
    kept = rows - SHIFT_R
    back = [
        halo(3, low_back.at[:kept], back_low.at[SHIFT_R:], after[1]),
        halo(4, low_back.at[kept:], back_low.at[:SHIFT_R], after[2]),
        halo(5, row_back, back_row, after[0]),
    ]
    pass_on(2, 2)
    pass_last(2, 0)
    for number in range(3, counts[2]):
        pass_on(2, number)
    pass_last(2, 1)
    for copy in back:
        copy.wait_recv()

    fine_ref[SHIFT_R:] = tok[SHIFT_R:].astype(f32) + attn[:kept]
    fine_ref[:SHIFT_R] = tok[:SHIFT_R].astype(f32) + back_row[...].astype(f32)
    fine_ref[:, :edge] = jnp.where(
        slot < near,
        tok[...].astype(f32)[:, :edge] + back_low[...].astype(f32),
        fine_ref[:, :edge],
    )

    group = cat.shape[0] // rows
    half_cols = slots // levels // 2
    lanes = 128
    for tile in range(width // lanes):
        split_fine[tile] = fine_ref[:, :, tile * lanes : (tile + 1) * lanes]
    for line in range(rows // 2):
        for level in range(levels):
            for part in range(4):
                start = levels * (part % 2) + level
                base = (line * levels + level) * group
                for tile in range(width // lanes):
                    place = part * width + tile * lanes
                    cat[base : base + half_cols, place : place + lanes] = split_fine[
                        tile, 2 * line + part // 2, pl.ds(start, half_cols, stride=2 * levels), :
                    ]
    for number in range(2, counts[2]):
        pass_last(2, number)
    cat_low[...] = layer_norm(cat[...]).astype(low_type)
    wide = merge_hbm.shape[1]

    def merge(owner):
        values = jnp.dot(cat_low[...], wm[owner], preferred_element_type=f32)
        place = pl.ds(pl.multiple_of(owner * wide, wide), wide)
        parts[:, place] = values.astype(low_type).astype(f32)

    own[2].wait()
    merge(row)
    across[2].wait_recv()
    merge(other_core)
    merge(other_chip)
    wait_far(2)
    merge(far)
    mid = parts.shape[1]
    for tile in range(mid // lanes):
        split_mid[tile] = parts[:, tile * lanes : (tile + 1) * lanes]
    quarter = half_cols // 2
    for line in range(rows // 4):
        for level in range(levels):
            for part in range(4):
                source = ((2 * line + part // 2) * levels + level) * group
                base = (line * levels + level) * quarter
                for tile in range(mid // lanes):
                    place = part * mid + tile * lanes
                    cat2[base : base + quarter, place : place + lanes] = split_mid[
                        tile, pl.ds(source + part % 2, quarter, stride=2), :
                    ]
    values = layer_norm(cat2[...]).astype(low_type)
    count, own_count, depth = blocks_ref.shape
    for index in range(count):
        blocks_ref[index] = values[:, index * depth : (index + 1) * depth]


    def drain():
        for copy in there + back:
            copy.wait_send()
        for copies in (over, across, first, second, third):
            for copy in copies.values():
                copy.wait_send()

    return drain


WEIGHT_PIECES = (2, 1, 4)


def count_up(values, size, total):
    found = jnp.zeros_like(values)
    for step in range(size, total, size):
        found += (values >= step).astype(jnp.int32)
    return found


def place_pieces(parts, pieces, mid_ref, half_rows, half_cols, levels):
    low, f32 = jnp.bfloat16, jnp.float32
    total, mid = mid_ref.shape
    held = parts.shape[0]
    group = held // (half_rows * levels)
    target = lax.broadcasted_iota(jnp.int32, (total, held), 0)
    source = lax.broadcasted_iota(jnp.int32, (total, held), 1)
    line = count_up(source, group, held)
    column = source - line * group
    row = count_up(line, levels, half_rows * levels)
    level = line - row * levels
    match = (target == (row * half_cols + column) * levels + level) & (column < half_cols)
    chosen = jnp.where(match, 1.0, 0.0).astype(low)
    mid_ref[...] = jnp.dot(chosen, parts[...].astype(low), preferred_element_type=f32)
    count, own_count, wide = pieces.shape
    quarter = half_cols // 2
    target = lax.broadcasted_iota(jnp.int32, (total, own_count), 0)
    source = lax.broadcasted_iota(jnp.int32, (total, own_count), 1)
    line = count_up(source, quarter, own_count)
    column = source - line * quarter
    row = count_up(line, levels, own_count)
    level = line - row * levels
    blocks = count // 4
    for part in range(4):
        place = ((2 * row + part // 2) * half_cols + 2 * column + part % 2) * levels + level
        chosen = jnp.where(target == place, 1.0, 0.0).astype(low)
        for block in range(blocks):
            cut = slice(block * wide, (block + 1) * wide)
            mid_ref[:, cut] += jnp.dot(
                chosen, pieces[part * blocks + block], preferred_element_type=f32
            )


def whole_kernel(attend_count, half_rows, half_cols, levels, *refs):
    ins, weights, outs, rest = refs[:4], refs[4:8], refs[8:10], refs[10:]
    fine_ref, mid_ref = outs
    blocks, pieces = rest[:2]
    attend_refs, coarse_refs = rest[2 : 2 + attend_count], rest[2 + attend_count :]
    load_sem = coarse_refs[18]

    def start_loads():
        for load in coarse_loads(weights, coarse_refs[:4], load_sem):
            load.start()

    drain = attend_kernel(*ins, fine_ref, blocks, *attend_refs, start_loads)
    coarse_steps(blocks, *weights, pieces, *coarse_refs)
    parts = attend_refs[PARTS_AT]
    place_pieces(parts, pieces, mid_ref, half_rows, half_cols, levels)
    drain()


PARTS_AT = 19


def whole_block(
    tokens, qkv_weight, proj_weight, merge_one, merge_two, mlp_in, mlp_out, split_weight
):
    rows, slots, width = tokens.shape
    low, f32 = jnp.bfloat16, jnp.float32
    levels = slots // (slots // 2)
    count = lax.axis_size("lon")
    near = levels * SHIFT_C
    edge = -(-near // 8) * 8
    half_cols = slots // levels // 2
    group = -(-half_cols // 8) * 8
    cats = rows // 2 * levels * group
    mid = 4 * merge_one.shape[1]
    own_count = rows // 4 * levels * (half_cols // 2)
    whole = pl.BlockSpec(memory_space=pltpu.VMEM)
    apart = pl.BlockSpec(memory_space=pl.ANY)
    tall = rows * slots
    depth = 4 * mid // count
    attend_scratch = [
        pltpu.VMEM((4,) + qkv_weight.shape, low),
        pltpu.VMEM((proj_weight.shape[0], 4 * proj_weight.shape[1]), low),
        pltpu.VMEM((4,) + merge_one.shape, low),
        pltpu.VMEM((rows, edge, width), low),
        pltpu.VMEM((SHIFT_R, slots, width), low),
        pltpu.VMEM((rows, edge, width), low),
        pltpu.VMEM((rows, slots, width), f32),
        pltpu.VMEM((tall, width), low),
        pltpu.VMEM((tall, 3 * width), low),
        pltpu.VMEM((WIN_R * slots, WIN_R * slots), f32),
        pltpu.VMEM((tall, width), low),
        pltpu.VMEM((rows, edge, width), low),
        pltpu.VMEM((SHIFT_R, slots, width), low),
        pltpu.VMEM((rows, slots, width), f32),
        pltpu.VMEM((SHIFT_R, slots, width), low),
        pltpu.VMEM((rows, edge, width), low),
        pltpu.VMEM((width // 128, rows, slots, 128), f32),
        pltpu.VMEM((cats, 4 * width), f32),
        pltpu.VMEM((cats, 4 * width), low),
        pltpu.VMEM((cats, mid), f32),
        pltpu.VMEM((mid // 128, cats, 128), f32),
        pltpu.VMEM((own_count, 4 * mid), f32),
        pltpu.SemaphoreType.DMA((6,)),
        pltpu.SemaphoreType.DMA((6,)),
        pltpu.SemaphoreType.DMA((3,)),
        pltpu.SemaphoreType.DMA((3, 5 * max(WEIGHT_PIECES))),
        pltpu.SemaphoreType.DMA((3, 5 * max(WEIGHT_PIECES))),
    ]
    return pl.pallas_call(
        functools.partial(
            whole_kernel, len(attend_scratch), rows // 2, half_cols, levels
        ),
        out_shape=[
            jax.ShapeDtypeStruct((rows, slots, width), f32),
            jax.ShapeDtypeStruct((rows // 2 * half_cols * levels, mid), f32),
        ],
        in_specs=[whole] + [apart] * 7,
        out_specs=[whole] * 2,
        scratch_shapes=[
            pltpu.VMEM((count, own_count, depth), low),
            pltpu.VMEM((count, own_count, split_weight.shape[1]), low),
        ]
        + attend_scratch
        + coarse_scratch(count, own_count, depth, merge_two, mlp_in, mlp_out, split_weight),
        compiler_params=pltpu.CompilerParams(
            collective_id=3, has_side_effects=True, vmem_limit_bytes=62 * 1024 * 1024
        ),
    )(
        tokens, qkv_weight, proj_weight, merge_one, merge_two, mlp_in, mlp_out, split_weight
    )


def on_any(
    fine_tokens, qkv_weight, proj_weight, merge_one, merge_two, mlp_in, mlp_out, split_weight
):
    levels, rows, cols, width = fine_tokens.shape
    lat_count = lax.axis_size("lat")
    head_dim = width // HEADS
    edges = (
        fine_tokens[:, :SHIFT_R, SHIFT_C:],
        fine_tokens[:, SHIFT_R:, :SHIFT_C],
        fine_tokens[:, :SHIFT_R, :SHIFT_C],
    )
    if lat_count == 4 and lax.axis_size("lon") % 2 == 0:
        row_came, col_came, both_came, full_qkv, full_proj = exchange(
            edges, -1, (qkv_weight, proj_weight), 1
        )
        merge_one, row_came = lax.optimization_barrier((merge_one, row_came))
        merge_far = lat_swap(merge_one, 2)
        merge_parts = (merge_one, lat_swap(merge_one, 1), merge_far, lat_swap(merge_far, 1))
    else:
        row_came, col_came, both_came = exchange(edges, -1, (), 1)
        full_qkv = lax.all_gather(qkv_weight, "lat", axis=1, tiled=True)
        full_proj = lax.all_gather(proj_weight, "lat", axis=1, tiled=True)
    upper = jnp.concatenate([fine_tokens[:, SHIFT_R:, SHIFT_C:], col_came], axis=2)
    lower = jnp.concatenate([row_came, both_came], axis=2)
    moved = jnp.concatenate([upper, lower], axis=1)
    normed = layer_norm(moved.astype(jnp.float32)).astype(jnp.bfloat16).reshape(-1, width)
    qkv = jnp.dot(normed, full_qkv, preferred_element_type=jnp.float32).astype(jnp.bfloat16)
    row_wins = rows // WIN_R
    col_wins = cols // WIN_C
    wins = row_wins * col_wins
    tokens = levels * WIN_R * WIN_C
    parts = qkv.reshape(levels, row_wins, WIN_R, col_wins, WIN_C, 3, HEADS, head_dim)
    parts = parts.transpose(1, 3, 0, 2, 4, 5, 6, 7).reshape(wins, tokens, 3, HEADS, head_dim)
    scores = jnp.einsum(
        "wqhd,wkhd->whqk", parts[:, :, 0], parts[:, :, 1], preferred_element_type=jnp.float32
    )
    scores = scores / math.sqrt(head_dim)
    global_rows = lax.axis_index("lat") * rows + jnp.arange(rows, dtype=jnp.int32)
    wrapped = (global_rows >= rows * lat_count - SHIFT_R).astype(jnp.int32).reshape(row_wins, WIN_R)
    labels = jnp.broadcast_to(
        wrapped[:, None, None, :, None], (row_wins, col_wins, levels, WIN_R, WIN_C)
    )
    labels = labels.reshape(wins, tokens)
    allowed = labels[:, :, None] == labels[:, None, :]
    scores = jnp.where(allowed[:, None], scores, jnp.float32(-1000000000.0))
    top = jnp.max(scores, axis=-1, keepdims=True)
    expo = jnp.exp(scores - top)
    probs = (expo / jnp.sum(expo, axis=-1, keepdims=True)).astype(jnp.bfloat16)
    heads_out = jnp.einsum(
        "whqk,wkhd->wqhd", probs, parts[:, :, 2], preferred_element_type=jnp.float32
    )
    heads_out = heads_out.astype(jnp.bfloat16).reshape(
        row_wins, col_wins, levels, WIN_R, WIN_C, width
    )
    heads_out = heads_out.transpose(2, 0, 3, 1, 4, 5).reshape(-1, width)
    attn = jnp.dot(heads_out, full_proj, preferred_element_type=jnp.float32).astype(jnp.bfloat16)
    attn = attn.reshape(levels, rows, cols, width)
    edges = (
        attn[:, rows - SHIFT_R :, : cols - SHIFT_C],
        attn[:, : rows - SHIFT_R, cols - SHIFT_C :],
        attn[:, rows - SHIFT_R :, cols - SHIFT_C :],
    )
    row_came, col_came, both_came = exchange(edges, 1, (), 2)
    upper = jnp.concatenate([both_came, row_came], axis=2)
    lower = jnp.concatenate([col_came, attn[:, : rows - SHIFT_R, : cols - SHIFT_C]], axis=2)
    back = jnp.concatenate([upper, lower], axis=1)
    fine_out = fine_tokens.astype(jnp.float32) + back.astype(jnp.float32)
    normed1 = layer_norm(cat_four(fine_out)).astype(jnp.bfloat16)
    if lat_count == 4 and lax.axis_size("lon") % 2 == 0:
        merged1 = in_owner_order(
            [
                jnp.dot(normed1, part, preferred_element_type=jnp.float32).astype(jnp.bfloat16)
                for part in merge_parts
            ]
        )
    else:
        merge_all = lax.all_gather(merge_one, "lat", axis=1, tiled=True)
        merged1 = jnp.dot(normed1, merge_all, preferred_element_type=jnp.float32)
        merged1 = merged1.astype(jnp.bfloat16)
    merged1 = merged1.reshape(levels, rows // 2, cols // 2, MID)
    normed2 = layer_norm(cat_four(merged1.astype(jnp.float32))).astype(jnp.bfloat16)
    pieces = coarse_apart(normed2, merge_two, mlp_in, mlp_out, split_weight)
    pieces = pieces.reshape(levels, rows // 4, cols // 4, 2, 2, MID).transpose(0, 1, 3, 2, 4, 5)
    pieces = pieces.reshape(levels, rows // 2, cols // 2, MID)
    mid_out = merged1.astype(jnp.float32) + pieces.astype(jnp.float32)
    return (fine_out, mid_out)


def on_device(
    fine_tokens, qkv_weight, proj_weight, merge_one, merge_two, mlp_in, mlp_out, split_weight
):
    levels, rows, cols, width = fine_tokens.shape
    lat_count, count = lax.axis_size("lat"), lax.axis_size("lon")
    fits = count % 4 == 0 and merge_two.shape[1] % (count * 128) == 0
    if lat_count != 4 or not fits or rows != 2 * WIN_R or cols != WIN_C or levels != 2:
        return on_any(
            fine_tokens, qkv_weight, proj_weight, merge_one, merge_two, mlp_in, mlp_out, split_weight
        )
    tokens = fine_tokens.transpose(1, 2, 0, 3).reshape(rows, cols * levels, width)
    fine, mid = whole_block(
        tokens, qkv_weight, proj_weight, merge_one, merge_two, mlp_in, mlp_out, split_weight
    )
    fine_out = fine.reshape(rows, cols, levels, width).transpose(2, 0, 1, 3)
    mid_out = mid.reshape(rows // 2, cols // 2, levels, MID).transpose(2, 0, 1, 3)
    return (fine_out, mid_out)


def solution(mesh):
    return jax.shard_map(
        on_device,
        mesh=mesh,
        in_specs=(
            P(None, "lat", "lon", None),
            P(None, "lat"),
            P(None, "lat"),
            P(None, "lat"),
            P("lon", None),
            P(None, "lon"),
            P("lon", None),
            P(None, "lon"),
        ),
        out_specs=(P(None, "lat", "lon", None), P(None, "lat", "lon", None)),
        check_vma=False,
    )
```

```python
import functools
import math

import jax
import jax.numpy as jnp
from jax import lax
from jax.experimental import pallas as pl
from jax.experimental.pallas import tpu as pltpu
from jax.sharding import PartitionSpec as P

MID = 1024
HEADS = 8
WIN_R = 6
WIN_C = 12
SHIFT_R = 3
SHIFT_C = 6


def layer_norm(values):
    centre = jnp.mean(values, axis=-1, keepdims=True)
    shifted = values - centre
    spread = jnp.mean(shifted * shifted, axis=-1, keepdims=True)
    return shifted * lax.rsqrt(spread + 1e-05)


def cat_four(grid):
    lev, rows, cols, width = grid.shape
    grid = grid.reshape(lev, rows // 2, 2, cols // 2, 2, width).transpose(0, 1, 3, 2, 4, 5)
    return grid.reshape(lev * (rows // 2) * (cols // 2), 4 * width)


def coarse_loads(sources, targets, sems):
    return [
        pltpu.make_async_copy(source, target, sems.at[index])
        for index, (source, target) in enumerate(zip(sources, targets))
    ]


def coarse_steps(
    blocks_ref, two_hbm, in_hbm, out_hbm, split_hbm, pieces_ref,
    two, w_in, w_out, split, landed, features, feat, y_sent, y_land, z_sent, z_land, held, own,
    gathered, normed, act, cols, sent3,
    load_sem, first_send, first_recv, y_send, y_recv, z_send, z_recv, g_send, g_recv, o_send,
    o_recv, last_send, last_recv,
):
    count = lax.axis_size("lon")
    me = lax.axis_index("lon")
    chips = count // 2
    z, y = me // 2, lax.rem(me, 2)
    partner = me + 1 - 2 * y
    own_count = blocks_ref.shape[1]
    width = own.shape[-1]
    low_type, f32 = jnp.bfloat16, jnp.float32
    loads = coarse_loads((two_hbm, in_hbm, out_hbm, split_hbm), (two, w_in, w_out, split), load_sem)
    far_first = list(range(2, chips)) + [1] if chips > 2 else list(range(1, chips))

    def level(step):
        return lax.rem(z + step, chips)

    def remote(source, target, sent, came, peer):
        return pltpu.make_async_remote_copy(
            src_ref=source,
            dst_ref=target,
            send_sem=sent,
            recv_sem=came,
            device_id={"lon": peer},
            device_id_type=pl.DeviceIdType.MESH,
        )

    def first_copy(peer, source):
        return remote(
            blocks_ref.at[peer],
            landed.at[lax.rem(source, 2), source // 2],
            first_send.at[peer],
            first_recv.at[source],
            peer,
        )

    def y_copy(phase, chunk, block):
        return remote(
            y_sent.at[phase, chunk, block],
            y_land.at[phase, chunk, block],
            y_send.at[phase, chunk, block],
            y_recv.at[phase, chunk, block],
            partner,
        )

    def z_copy(phase, chunk, to, source):
        return remote(
            z_sent.at[phase, chunk, to],
            z_land.at[phase, chunk, source],
            z_send.at[phase, chunk, to],
            z_recv.at[phase, chunk, source],
            to * 2 + y,
        )

    def g_copy(phase, chunk, to, source):
        place = gathered.at[phase, chunk, source * 2 + y]
        return remote(
            place, place, g_send.at[phase, chunk, to], g_recv.at[phase, chunk, source], to * 2 + y
        )

    def o_copy(phase, chunk, block, side):
        place = gathered.at[phase, chunk, block * 2 + side]
        return remote(
            place, place, o_send.at[phase, chunk, block], o_recv.at[phase, chunk, block], partner
        )

    def last_copy(peer, source):
        return remote(
            sent3.at[lax.rem(peer, 2), peer // 2],
            pieces_ref.at[source],
            last_send.at[peer],
            last_recv.at[source],
            peer,
        )

    def product(left, weight, peer):
        cut = pl.ds(pl.multiple_of(peer * width, width), width)
        return jnp.dot(left[...], weight[:, cut], preferred_element_type=f32)

    def start_y(phase, chunk, left, weight):
        for step in far_first + [0]:
            block = level(step)
            y_sent[phase, chunk, block] = product(left, weight, block * 2 + 1 - y).astype(low_type)
            y_copy(phase, chunk, block).start()

    def hold(chunk, left, weight):
        for step in far_first + [0]:
            block = level(step)
            held[chunk, block] = product(left, weight, block * 2 + y)

    def start_z(phase, chunk):
        for step in far_first:
            block = level(step)
            y_copy(phase, chunk, block).wait_recv()
            total = held[chunk, block] + y_land[phase, chunk, block].astype(f32)
            z_sent[phase, chunk, block] = total.astype(low_type)
            z_copy(phase, chunk, block, z).start()

    def finish(phase, chunk):
        y_copy(phase, chunk, z).wait_recv()
        total = held[chunk, z] + y_land[phase, chunk, z].astype(f32)
        for step in range(1, chips):
            block = level(step)
            z_copy(phase, chunk, block, block).wait_recv()
            total = total + z_land[phase, chunk, block].astype(f32)
        return total

    def spread(phase, chunk, values):
        gathered[phase, chunk, me] = values.astype(low_type)
        for step in far_first:
            g_copy(phase, chunk, level(step), z).start()
        o_copy(phase, chunk, z, y).start()

    def forward(phase, chunk):
        for step in range(1, chips):
            block = level(step)
            g_copy(phase, chunk, block, block).wait_recv()
            o_copy(phase, chunk, block, y).start()

    def arrive(phase, chunk):
        for step in range(chips):
            o_copy(phase, chunk, level(step), 1 - y).wait_recv()

    for step in range(1, count):
        first_copy(lax.rem(me + step, count), me).start()
    landed[y, z] = blocks_ref[me]
    chunks = (0, 1)
    for chunk in chunks:
        for index in range(chips):
            source = index * 2 + chunk
            pl.when(source != me)(lambda: first_copy(source, source).wait_recv())
        for index in range(chips):
            features[index * own_count : (index + 1) * own_count] = landed[chunk, index].astype(f32)
        feat[chunk] = features[...].astype(low_type)
        if chunk == 0:
            loads[0].wait()
        start_y(0, chunk, feat.at[chunk], two)
    for chunk in chunks:
        hold(chunk, feat.at[chunk], two)
        start_z(0, chunk)
    for chunk in chunks:
        merged = finish(0, chunk)
        own[chunk] = merged
        spread(0, chunk, merged)
    loads[1].wait()
    loads[2].wait()
    total_width = count * width
    tile = min(256, act.shape[-1])
    for chunk in chunks:
        forward(0, chunk)
    for chunk in chunks:
        arrive(0, chunk)
        centre = gathered[0, chunk, 0].astype(f32).sum(axis=-1, keepdims=True)
        for index in range(1, count):
            centre += gathered[0, chunk, index].astype(f32).sum(axis=-1, keepdims=True)
        centre = centre / total_width
        spread_sum = jnp.zeros_like(centre)
        for index in range(count):
            shifted = gathered[0, chunk, index].astype(f32) - centre
            spread_sum += (shifted * shifted).sum(axis=-1, keepdims=True)
        scale = lax.rsqrt(spread_sum / total_width + 1e-05)
        for index in range(count):
            shifted = gathered[0, chunk, index].astype(f32) - centre
            normed[chunk, :, index * width : (index + 1) * width] = (shifted * scale).astype(
                low_type
            )

        def hidden(index, carry):
            cut = pl.ds(pl.multiple_of(index * tile, tile), tile)
            values = jnp.dot(normed[chunk], w_in[:, cut], preferred_element_type=f32)
            act[chunk, :, cut] = jax.nn.gelu(values).astype(low_type)
            return carry

        lax.fori_loop(0, act.shape[-1] // tile, hidden, 0, unroll=True)
        start_y(1, chunk, act.at[chunk], w_out)
    for chunk in chunks:
        hold(chunk, act.at[chunk], w_out)
        start_z(1, chunk)
    for chunk in chunks:
        spread(1, chunk, own[chunk] + finish(1, chunk))
    for chunk in chunks:
        forward(1, chunk)
    loads[3].wait()
    for chunk in chunks:
        arrive(1, chunk)
        for index in range(count):
            normed[chunk, :, index * width : (index + 1) * width] = gathered[1, chunk, index]
        cols[...] = jnp.dot(normed[chunk], split[...], preferred_element_type=f32)
        for index in range(chips):
            values = cols[index * own_count : (index + 1) * own_count]
            sent3[chunk, index] = values.astype(low_type)
        for step in range(chips):
            peer = level(step) * 2 + chunk
            pl.when(peer != me)(lambda: last_copy(peer, me).start())
    pieces_ref[me] = sent3[y, z]
    for step in range(1, count):
        source = lax.rem(me + step, count)
        last_copy(source, source).wait_recv()
    for step in range(1, count):
        peer = lax.rem(me + step, count)
        first_copy(peer, me).wait_send()
        last_copy(peer, me).wait_send()
    for phase in (0, 1):
        for chunk in chunks:
            for step in range(chips):
                y_copy(phase, chunk, level(step)).wait_send()
                o_copy(phase, chunk, level(step), y).wait_send()
                if step > 0:
                    z_copy(phase, chunk, level(step), z).wait_send()
                    g_copy(phase, chunk, level(step), z).wait_send()


def coarse_scratch(count, own_count, depth, merge_two, mlp_in, mlp_out, split_weight):
    low, f32 = jnp.bfloat16, jnp.float32
    chips = count // 2
    tokens, top = chips * own_count, merge_two.shape[1]
    width, hidden, split_width = top // count, mlp_in.shape[1], split_weight.shape[1]
    dma = pltpu.SemaphoreType.DMA
    return [
        pltpu.VMEM(merge_two.shape, low),
        pltpu.VMEM(mlp_in.shape, low),
        pltpu.VMEM(mlp_out.shape, low),
        pltpu.VMEM(split_weight.shape, low),
        pltpu.VMEM((2, chips, own_count, depth), low),
        pltpu.VMEM((tokens, depth), f32),
        pltpu.VMEM((2, tokens, depth), low),
        pltpu.VMEM((2, 2, chips, tokens, width), low),
        pltpu.VMEM((2, 2, chips, tokens, width), low),
        pltpu.VMEM((2, 2, chips, tokens, width), low),
        pltpu.VMEM((2, 2, chips, tokens, width), low),
        pltpu.VMEM((2, chips, tokens, width), f32),
        pltpu.VMEM((2, tokens, width), f32),
        pltpu.VMEM((2, 2, count, tokens, width), low),
        pltpu.VMEM((2, tokens, top), low),
        pltpu.VMEM((2, tokens, hidden), low),
        pltpu.VMEM((tokens, split_width), f32),
        pltpu.VMEM((2, chips, own_count, split_width), low),
        dma((4,)),
        dma((count,)),
        dma((count,)),
    ] + [dma((2, 2, chips)) for _ in range(8)] + [dma((count,)), dma((count,))]


def coarse_apart(normed2, merge_two, mlp_in, mlp_out, split_weight):
    own_count = normed2.shape[0]
    feature_parts = lax.all_to_all(normed2, "lon", split_axis=1, concat_axis=0, tiled=True)
    partial_value = jnp.dot(feature_parts, merge_two, preferred_element_type=jnp.float32)
    merged2 = lax.psum(partial_value.astype(jnp.bfloat16), "lon").astype(jnp.float32)
    normed3 = layer_norm(merged2).astype(jnp.bfloat16)
    act = jax.nn.gelu(jnp.dot(normed3, mlp_in, preferred_element_type=jnp.float32)).astype(
        jnp.bfloat16
    )
    mlp_own = lax.psum_scatter(
        jnp.dot(act, mlp_out, preferred_element_type=jnp.float32).astype(jnp.bfloat16),
        "lon",
        scatter_dimension=0,
        tiled=True,
    ).astype(jnp.float32)
    own_merged = lax.dynamic_slice_in_dim(merged2, lax.axis_index("lon") * own_count, own_count, 0)
    coarse = (own_merged + mlp_own).astype(jnp.bfloat16)
    split_cols = jnp.dot(
        lax.all_gather(coarse, "lon", axis=0, tiled=True),
        split_weight,
        preferred_element_type=jnp.float32,
    ).astype(jnp.bfloat16)
    return lax.all_to_all(split_cols, "lon", split_axis=0, concat_axis=1, tiled=True)


def halo_kernel(direction, shards, *refs):
    edges, weights = refs[:3], refs[3 : 3 + shards]
    came, wholes = refs[3 + shards : 6 + shards], refs[6 + shards : 6 + 2 * shards]
    edge_send, edge_recv, own_sem, weight_send, weight_recv = refs[6 + 2 * shards :]
    lat_count, lon_count = lax.axis_size("lat"), lax.axis_size("lon")
    row, col = lax.axis_index("lat"), lax.axis_index("lon")
    mesh = pl.DeviceIdType.MESH

    def beside(sign):
        next_row = lax.rem(row + sign + lat_count, lat_count)
        next_col = lax.rem(col + sign + lon_count, lon_count)
        return (next_row, col), (row, next_col), (next_row, next_col)

    other_core = row + 1 - 2 * lax.rem(row, 2)
    other_chip = lax.rem(row + 2, 4)
    side = lax.rem(col, 2)
    pair = col + 1 - 2 * side
    partners = beside(1) + beside(-1)
    if shards:
        partners += ((other_core, col), (other_chip, col), (row, pair))
    barrier = pltpu.get_barrier_semaphore()
    for partner in partners:
        pl.semaphore_signal(barrier, inc=1, device_id=partner, device_id_type=mesh)
    pl.semaphore_wait(barrier, len(partners))

    copies = []
    for index, target in enumerate(beside(direction)):
        copies.append(
            pltpu.make_async_remote_copy(
                src_ref=edges[index],
                dst_ref=came[index],
                send_sem=edge_send.at[index],
                recv_sem=edge_recv.at[index],
                device_id=target,
                device_id_type=mesh,
            )
        )
    for copy in copies:
        copy.start()

    def columns(index, owner):
        width = weights[index].shape[1]
        return wholes[index].at[:, pl.ds(pl.multiple_of(owner * width, width), width)]

    def half(ref, index, which):
        depth = weights[index].shape[0] // 2
        return ref.at[pl.ds(pl.multiple_of(which * depth, depth), depth)]

    def send(index, kind, source, target, device):
        copy = pltpu.make_async_remote_copy(
            src_ref=source,
            dst_ref=target,
            send_sem=weight_send.at[index, kind],
            recv_sem=weight_recv.at[index, kind],
            device_id=device,
            device_id_type=mesh,
        )
        copy.start()
        return copy

    moves = []
    for index in range(shards):
        mine, held = weights[index], columns(index, row)
        away = send(
            index, 0, half(mine, index, side), half(held, index, side), (other_chip, col)
        )
        moves.append([away, send(index, 1, mine, held, (other_core, col))])
        pltpu.make_async_copy(mine, held, own_sem.at[index]).start()
    for index in range(shards):
        moves[index][0].wait_recv()
        part = half(columns(index, other_chip), index, side)
        moves[index].append(send(index, 2, part, part, (row, pair)))
        moves[index].append(send(index, 3, part, part, (other_core, col)))
    for index in range(shards):
        moves[index][2].wait_recv()
        part = half(columns(index, other_chip), index, 1 - side)
        moves[index].append(send(index, 4, part, part, (other_core, col)))
    for index in range(shards):
        away, core, paired, first, second = moves[index]
        for copy in (away, core, paired, first, second):
            copy.wait_send()
        for copy in (core, first, second):
            copy.wait_recv()
        pltpu.make_async_copy(weights[index], columns(index, row), own_sem.at[index]).wait()
    for copy in copies:
        copy.wait()


def exchange(edges, direction, weights, identity):
    whole = pl.BlockSpec(memory_space=pltpu.VMEM)
    shards = len(weights)
    outs = [jax.ShapeDtypeStruct(edge.shape, edge.dtype) for edge in edges]
    outs += [
        jax.ShapeDtypeStruct((part.shape[0], 4 * part.shape[1]), part.dtype) for part in weights
    ]
    return pl.pallas_call(
        functools.partial(halo_kernel, direction, shards),
        out_shape=outs,
        in_specs=[whole] * (3 + shards),
        out_specs=[whole] * (3 + shards),
        scratch_shapes=[
            pltpu.SemaphoreType.DMA((3,)),
            pltpu.SemaphoreType.DMA((3,)),
            pltpu.SemaphoreType.DMA((max(shards, 1),)),
            pltpu.SemaphoreType.DMA((max(shards, 1), 5)),
            pltpu.SemaphoreType.DMA((max(shards, 1), 5)),
        ],
        compiler_params=pltpu.CompilerParams(collective_id=identity, has_side_effects=True),
    )(*edges, *weights)


def lat_swap(value, mask):
    return lax.ppermute(value, "lat", [(index, index ^ mask) for index in range(4)])


def in_owner_order(parts):
    index = lax.axis_index("lat")
    odd, high = index % 2 == 1, index >= 2
    a, b, c, d = parts
    a, b = jnp.where(odd, b, a), jnp.where(odd, a, b)
    c, d = jnp.where(odd, d, c), jnp.where(odd, c, d)
    a, c = jnp.where(high, c, a), jnp.where(high, a, c)
    b, d = jnp.where(high, d, b), jnp.where(high, b, d)
    return jnp.concatenate((a, b, c, d), axis=-1)


def attend_kernel(
    tok, qkv_hbm, proj_hbm, merge_hbm, fine_ref, blocks_ref,
    wq, wp, wm, low, came_row, came_low, packed, normed, qkv, bias, heads, low_back, row_back,
    attn, back_row, back_low, split_fine, cat, cat_low, parts, split_mid, cat2,
    halo_send, halo_recv, own_sem, weight_send, weight_recv, start_loads,
):
    lat_count, lon_count = lax.axis_size("lat"), lax.axis_size("lon")
    row, col = lax.axis_index("lat"), lax.axis_index("lon")
    mesh = pl.DeviceIdType.MESH
    f32, low_type = jnp.float32, jnp.bfloat16
    rows, slots, width = tok.shape
    levels = 2
    near = levels * SHIFT_C
    edge = low.shape[1]
    head_dim = width // HEADS

    def beside(sign):
        next_row = lax.rem(row + sign + lat_count, lat_count)
        next_col = lax.rem(col + sign + lon_count, lon_count)
        return (next_row, col), (row, next_col), (next_row, next_col)

    other_core = row + 1 - 2 * lax.rem(row, 2)
    other_chip = lax.rem(row + 2, 4)
    far = lax.rem(other_core + 2, 4)
    side = lax.rem(col, 2)
    pair = col + 1 - 2 * side
    high_side = lax.rem(col // 2, 2)
    high_pair = col + 2 - 4 * high_side
    sides, pairs = (side, side, high_side), (pair, pair, high_pair)
    low[...] = tok[...].astype(f32)[:, :edge].astype(low_type)
    cat[...] = jnp.zeros_like(cat)
    partners = beside(1) + beside(-1) + ((other_core, col), (other_chip, col))
    partners += tuple((row, lax.rem(col + step, lon_count)) for step in range(1, lon_count))
    barrier = pltpu.get_barrier_semaphore()
    for partner in partners:
        pl.semaphore_signal(barrier, inc=1, device_id=partner, device_id_type=mesh)
    pl.semaphore_wait(barrier, len(partners))

    shards = (qkv_hbm, proj_hbm, merge_hbm)
    counts = WEIGHT_PIECES

    def whole(index, owner):
        if index == 1:
            cut = proj_hbm.shape[1]
            return wp.at[:, pl.ds(pl.multiple_of(owner * cut, cut), cut)]
        return (wq if index == 0 else wm).at[owner]

    def piece(ref, index, which, number):
        depth = shards[index].shape[0] // 2
        size = depth // counts[index]
        start = pl.multiple_of(which * depth + number * size, size)
        return ref.at[pl.ds(start, size)]

    def send(index, kind, number, source, target, device):
        place = kind * max(counts) + number
        copy = pltpu.make_async_remote_copy(
            src_ref=source,
            dst_ref=target,
            send_sem=weight_send.at[index, place],
            recv_sem=weight_recv.at[index, place],
            device_id=device,
            device_id_type=mesh,
        )
        copy.start()
        return copy

    over, across, own = {}, {}, {}
    first, second, third = {}, {}, {}

    def send_over(index):
        for number in range(counts[index]):
            over[index, number] = send(
                index, 0, number,
                piece(shards[index], index, sides[index], number),
                piece(whole(index, row), index, sides[index], number),
                (other_chip, col),
            )

    def send_across(index):
        across[index] = send(
            index, 1, 0, shards[index], whole(index, row), (other_core, col)
        )
        own[index] = pltpu.make_async_copy(shards[index], whole(index, row), own_sem.at[index])
        own[index].start()

    def pass_on(index, number):
        over[index, number].wait_recv()
        held = piece(whole(index, other_chip), index, sides[index], number)
        first[index, number] = send(index, 2, number, held, held, (row, pairs[index]))
        second[index, number] = send(index, 3, number, held, held, (other_core, col))

    def pass_last(index, number):
        first[index, number].wait_recv()
        held = piece(whole(index, other_chip), index, 1 - sides[index], number)
        third[index, number] = send(index, 4, number, held, held, (other_core, col))

    def wait_far(index):
        for number in range(counts[index]):
            second[index, number].wait_recv()
            third[index, number].wait_recv()

    def halo(place, source, target, device):
        copy = pltpu.make_async_remote_copy(
            src_ref=source,
            dst_ref=target,
            send_sem=halo_send.at[place],
            recv_sem=halo_recv.at[place],
            device_id=device,
            device_id_type=mesh,
        )
        copy.start()
        return copy

    before, after = beside(-1), beside(1)
    there = [
        halo(0, low.at[SHIFT_R:], came_low.at[SHIFT_R:], before[1]),
        halo(1, low.at[:SHIFT_R], came_low.at[:SHIFT_R], before[2]),
    ]
    there.append(halo(2, tok.at[:SHIFT_R], came_row, before[0]))
    send_over(0)
    send_across(0)
    send_over(1)
    send_across(1)
    send_over(2)
    send_across(2)
    start_loads()

    slot = lax.broadcasted_iota(jnp.int32, (1, edge, width), 1)
    tokens = WIN_R * slots
    wins = rows // WIN_R
    key_row = lax.broadcasted_iota(jnp.int32, (tokens, tokens), 1) >= (WIN_R - SHIFT_R) * slots
    query_row = lax.broadcasted_iota(jnp.int32, (tokens, tokens), 0) >= (WIN_R - SHIFT_R) * slots
    last = jnp.where(row == lat_count - 1, f32(-1000000000.0), f32(0.0))
    bias[...] = jnp.where(key_row == query_row, f32(0.0), last)

    for number in range(counts[0]):
        pass_on(0, number)
    for copy in there:
        copy.wait_recv()
    packed[: rows - SHIFT_R] = tok[SHIFT_R:].astype(f32)
    packed[rows - SHIFT_R :] = came_row[...].astype(f32)
    packed[: rows - SHIFT_R, :edge] = jnp.where(
        slot < near, came_low[SHIFT_R:].astype(f32), packed[: rows - SHIFT_R, :edge]
    )
    packed[rows - SHIFT_R :, :edge] = jnp.where(
        slot < near, came_low[:SHIFT_R].astype(f32), packed[rows - SHIFT_R :, :edge]
    )
    for win in range(wins):
        values = packed[win * WIN_R : (win + 1) * WIN_R].reshape(tokens, width)
        normed[win * tokens : (win + 1) * tokens] = layer_norm(values).astype(low_type)

    cut = qkv_hbm.shape[1]

    def project(owner):
        place = pl.ds(pl.multiple_of(owner * cut, cut), cut)
        qkv[:, place] = jnp.dot(
            normed[...], wq[owner], preferred_element_type=f32
        ).astype(low_type)

    own[0].wait()
    project(row)
    across[0].wait_recv()
    project(other_core)
    for number in range(counts[0]):
        pass_last(0, number)
    project(other_chip)
    wait_far(0)
    project(far)

    for number in range(counts[1]):
        pass_on(1, number)
    pass_on(2, 0)

    lane = lax.broadcasted_iota(jnp.int32, (1, 2 * head_dim), 1)
    near_head = jnp.where(lane < head_dim, 1.0, 0.0).astype(low_type)
    scale = 1.0 / math.sqrt(head_dim)

    def attend(win):
        place = pl.ds(win * tokens, tokens)

        def head_pair(index, carry):
            def columns(kind):
                start = pl.multiple_of(kind * width + index * 2 * head_dim, 2 * head_dim)
                return qkv[place, pl.ds(start, 2 * head_dim)]

            query, key, value = columns(0), columns(1), columns(2)
            outs = []
            for mask in (near_head, 1 - near_head):
                scores = lax.dot_general(
                    query, key * mask, (((1,), (1,)), ((), ())), preferred_element_type=f32
                )
                scores = scores * scale
                if win == wins - 1:
                    scores = scores + bias[...]
                expo = jnp.exp(scores - jnp.max(scores, axis=-1, keepdims=True))
                total = jnp.sum(expo, axis=-1, keepdims=True)
                out = jnp.dot(expo.astype(low_type), value, preferred_element_type=f32)
                outs.append(out / total)
            start = pl.multiple_of(index * 2 * head_dim, 2 * head_dim)
            heads[place, pl.ds(start, 2 * head_dim)] = jnp.where(
                lane < head_dim, outs[0], outs[1]
            ).astype(low_type)
            return carry

        lax.fori_loop(0, HEADS // 2, head_pair, 0, unroll=True)

    for win in range(wins):
        attend(win)
        if win == 0:
            pass_on(2, 1)

    for number in range(counts[1]):
        pass_last(1, number)
    own[1].wait()
    across[1].wait_recv()
    wait_far(1)
    for win in range(wins):
        values = jnp.dot(
            heads[win * tokens : (win + 1) * tokens], wp[...], preferred_element_type=f32
        )
        values = values.astype(low_type).astype(f32).reshape(WIN_R, slots, width)
        attn[win * WIN_R : (win + 1) * WIN_R] = values
    low_back[...] = attn[:, :edge].astype(low_type)
    row_back[...] = attn[rows - SHIFT_R :].astype(low_type)
    kept = rows - SHIFT_R
    back = [
        halo(3, low_back.at[:kept], back_low.at[SHIFT_R:], after[1]),
        halo(4, low_back.at[kept:], back_low.at[:SHIFT_R], after[2]),
        halo(5, row_back, back_row, after[0]),
    ]
    pass_on(2, 2)
    pass_last(2, 0)
    for number in range(3, counts[2]):
        pass_on(2, number)
    pass_last(2, 1)
    for copy in back:
        copy.wait_recv()

    fine_ref[SHIFT_R:] = tok[SHIFT_R:].astype(f32) + attn[:kept]
    fine_ref[:SHIFT_R] = tok[:SHIFT_R].astype(f32) + back_row[...].astype(f32)
    fine_ref[:, :edge] = jnp.where(
        slot < near,
        tok[...].astype(f32)[:, :edge] + back_low[...].astype(f32),
        fine_ref[:, :edge],
    )

    group = cat.shape[0] // rows
    half_cols = slots // levels // 2
    lanes = 128
    for tile in range(width // lanes):
        split_fine[tile] = fine_ref[:, :, tile * lanes : (tile + 1) * lanes]
    for line in range(rows // 2):
        for level in range(levels):
            for part in range(4):
                start = levels * (part % 2) + level
                base = (line * levels + level) * group
                for tile in range(width // lanes):
                    place = part * width + tile * lanes
                    cat[base : base + half_cols, place : place + lanes] = split_fine[
                        tile, 2 * line + part // 2, pl.ds(start, half_cols, stride=2 * levels), :
                    ]
    for number in range(2, counts[2]):
        pass_last(2, number)
    cat_low[...] = layer_norm(cat[...]).astype(low_type)
    wide = merge_hbm.shape[1]

    def merge(owner):
        values = jnp.dot(cat_low[...], wm[owner], preferred_element_type=f32)
        place = pl.ds(pl.multiple_of(owner * wide, wide), wide)
        parts[:, place] = values.astype(low_type).astype(f32)

    own[2].wait()
    merge(row)
    across[2].wait_recv()
    merge(other_core)
    merge(other_chip)
    wait_far(2)
    merge(far)
    mid = parts.shape[1]
    for tile in range(mid // lanes):
        split_mid[tile] = parts[:, tile * lanes : (tile + 1) * lanes]
    quarter = half_cols // 2
    for line in range(rows // 4):
        for level in range(levels):
            for part in range(4):
                source = ((2 * line + part // 2) * levels + level) * group
                base = (line * levels + level) * quarter
                for tile in range(mid // lanes):
                    place = part * mid + tile * lanes
                    cat2[base : base + quarter, place : place + lanes] = split_mid[
                        tile, pl.ds(source + part % 2, quarter, stride=2), :
                    ]
    values = layer_norm(cat2[...]).astype(low_type)
    count, own_count, depth = blocks_ref.shape
    for index in range(count):
        blocks_ref[index] = values[:, index * depth : (index + 1) * depth]


    def drain():
        for copy in there + back:
            copy.wait_send()
        for copies in (over, across, first, second, third):
            for copy in copies.values():
                copy.wait_send()

    return drain


WEIGHT_PIECES = (2, 1, 4)


def count_up(values, size, total):
    found = jnp.zeros_like(values)
    for step in range(size, total, size):
        found += (values >= step).astype(jnp.int32)
    return found


def place_pieces(parts, pieces, mid_ref, half_rows, half_cols, levels):
    low, f32 = jnp.bfloat16, jnp.float32
    total, mid = mid_ref.shape
    held = parts.shape[0]
    group = held // (half_rows * levels)
    target = lax.broadcasted_iota(jnp.int32, (total, held), 0)
    source = lax.broadcasted_iota(jnp.int32, (total, held), 1)
    line = count_up(source, group, held)
    column = source - line * group
    row = count_up(line, levels, half_rows * levels)
    level = line - row * levels
    match = (target == (row * half_cols + column) * levels + level) & (column < half_cols)
    chosen = jnp.where(match, 1.0, 0.0).astype(low)
    mid_ref[...] = jnp.dot(chosen, parts[...].astype(low), preferred_element_type=f32)
    count, own_count, wide = pieces.shape
    quarter = half_cols // 2
    target = lax.broadcasted_iota(jnp.int32, (total, own_count), 0)
    source = lax.broadcasted_iota(jnp.int32, (total, own_count), 1)
    line = count_up(source, quarter, own_count)
    column = source - line * quarter
    row = count_up(line, levels, own_count)
    level = line - row * levels
    blocks = count // 4
    for part in range(4):
        place = ((2 * row + part // 2) * half_cols + 2 * column + part % 2) * levels + level
        chosen = jnp.where(target == place, 1.0, 0.0).astype(low)
        for block in range(blocks):
            cut = slice(block * wide, (block + 1) * wide)
            mid_ref[:, cut] += jnp.dot(
                chosen, pieces[part * blocks + block], preferred_element_type=f32
            )


def whole_kernel(attend_count, half_rows, half_cols, levels, *refs):
    ins, weights, outs, rest = refs[:4], refs[4:8], refs[8:10], refs[10:]
    fine_ref, mid_ref = outs
    blocks, pieces = rest[:2]
    attend_refs, coarse_refs = rest[2 : 2 + attend_count], rest[2 + attend_count :]
    load_sem = coarse_refs[18]

    def start_loads():
        for load in coarse_loads(weights, coarse_refs[:4], load_sem):
            load.start()

    drain = attend_kernel(*ins, fine_ref, blocks, *attend_refs, start_loads)
    coarse_steps(blocks, *weights, pieces, *coarse_refs)
    parts = attend_refs[PARTS_AT]
    place_pieces(parts, pieces, mid_ref, half_rows, half_cols, levels)
    drain()


PARTS_AT = 19


def whole_block(
    tokens, qkv_weight, proj_weight, merge_one, merge_two, mlp_in, mlp_out, split_weight
):
    rows, slots, width = tokens.shape
    low, f32 = jnp.bfloat16, jnp.float32
    levels = slots // (slots // 2)
    count = lax.axis_size("lon")
    near = levels * SHIFT_C
    edge = -(-near // 8) * 8
    half_cols = slots // levels // 2
    group = -(-half_cols // 8) * 8
    cats = rows // 2 * levels * group
    mid = 4 * merge_one.shape[1]
    own_count = rows // 4 * levels * (half_cols // 2)
    whole = pl.BlockSpec(memory_space=pltpu.VMEM)
    apart = pl.BlockSpec(memory_space=pl.ANY)
    tall = rows * slots
    depth = 4 * mid // count
    attend_scratch = [
        pltpu.VMEM((4,) + qkv_weight.shape, low),
        pltpu.VMEM((proj_weight.shape[0], 4 * proj_weight.shape[1]), low),
        pltpu.VMEM((4,) + merge_one.shape, low),
        pltpu.VMEM((rows, edge, width), low),
        pltpu.VMEM((SHIFT_R, slots, width), low),
        pltpu.VMEM((rows, edge, width), low),
        pltpu.VMEM((rows, slots, width), f32),
        pltpu.VMEM((tall, width), low),
        pltpu.VMEM((tall, 3 * width), low),
        pltpu.VMEM((WIN_R * slots, WIN_R * slots), f32),
        pltpu.VMEM((tall, width), low),
        pltpu.VMEM((rows, edge, width), low),
        pltpu.VMEM((SHIFT_R, slots, width), low),
        pltpu.VMEM((rows, slots, width), f32),
        pltpu.VMEM((SHIFT_R, slots, width), low),
        pltpu.VMEM((rows, edge, width), low),
        pltpu.VMEM((width // 128, rows, slots, 128), f32),
        pltpu.VMEM((cats, 4 * width), f32),
        pltpu.VMEM((cats, 4 * width), low),
        pltpu.VMEM((cats, mid), f32),
        pltpu.VMEM((mid // 128, cats, 128), f32),
        pltpu.VMEM((own_count, 4 * mid), f32),
        pltpu.SemaphoreType.DMA((6,)),
        pltpu.SemaphoreType.DMA((6,)),
        pltpu.SemaphoreType.DMA((3,)),
        pltpu.SemaphoreType.DMA((3, 5 * max(WEIGHT_PIECES))),
        pltpu.SemaphoreType.DMA((3, 5 * max(WEIGHT_PIECES))),
    ]
    return pl.pallas_call(
        functools.partial(
            whole_kernel, len(attend_scratch), rows // 2, half_cols, levels
        ),
        out_shape=[
            jax.ShapeDtypeStruct((rows, slots, width), f32),
            jax.ShapeDtypeStruct((rows // 2 * half_cols * levels, mid), f32),
        ],
        in_specs=[whole] + [apart] * 7,
        out_specs=[whole] * 2,
        scratch_shapes=[
            pltpu.VMEM((count, own_count, depth), low),
            pltpu.VMEM((count, own_count, split_weight.shape[1]), low),
        ]
        + attend_scratch
        + coarse_scratch(count, own_count, depth, merge_two, mlp_in, mlp_out, split_weight),
        compiler_params=pltpu.CompilerParams(
            collective_id=3, has_side_effects=True, vmem_limit_bytes=52 * 1024 * 1024
        ),
    )(
        tokens, qkv_weight, proj_weight, merge_one, merge_two, mlp_in, mlp_out, split_weight
    )


def on_any(
    fine_tokens, qkv_weight, proj_weight, merge_one, merge_two, mlp_in, mlp_out, split_weight
):
    levels, rows, cols, width = fine_tokens.shape
    lat_count = lax.axis_size("lat")
    head_dim = width // HEADS
    edges = (
        fine_tokens[:, :SHIFT_R, SHIFT_C:],
        fine_tokens[:, SHIFT_R:, :SHIFT_C],
        fine_tokens[:, :SHIFT_R, :SHIFT_C],
    )
    if lat_count == 4 and lax.axis_size("lon") % 2 == 0:
        row_came, col_came, both_came, full_qkv, full_proj = exchange(
            edges, -1, (qkv_weight, proj_weight), 1
        )
        merge_one, row_came = lax.optimization_barrier((merge_one, row_came))
        merge_far = lat_swap(merge_one, 2)
        merge_parts = (merge_one, lat_swap(merge_one, 1), merge_far, lat_swap(merge_far, 1))
    else:
        row_came, col_came, both_came = exchange(edges, -1, (), 1)
        full_qkv = lax.all_gather(qkv_weight, "lat", axis=1, tiled=True)
        full_proj = lax.all_gather(proj_weight, "lat", axis=1, tiled=True)
    upper = jnp.concatenate([fine_tokens[:, SHIFT_R:, SHIFT_C:], col_came], axis=2)
    lower = jnp.concatenate([row_came, both_came], axis=2)
    moved = jnp.concatenate([upper, lower], axis=1)
    normed = layer_norm(moved.astype(jnp.float32)).astype(jnp.bfloat16).reshape(-1, width)
    qkv = jnp.dot(normed, full_qkv, preferred_element_type=jnp.float32).astype(jnp.bfloat16)
    row_wins = rows // WIN_R
    col_wins = cols // WIN_C
    wins = row_wins * col_wins
    tokens = levels * WIN_R * WIN_C
    parts = qkv.reshape(levels, row_wins, WIN_R, col_wins, WIN_C, 3, HEADS, head_dim)
    parts = parts.transpose(1, 3, 0, 2, 4, 5, 6, 7).reshape(wins, tokens, 3, HEADS, head_dim)
    scores = jnp.einsum(
        "wqhd,wkhd->whqk", parts[:, :, 0], parts[:, :, 1], preferred_element_type=jnp.float32
    )
    scores = scores / math.sqrt(head_dim)
    global_rows = lax.axis_index("lat") * rows + jnp.arange(rows, dtype=jnp.int32)
    wrapped = (global_rows >= rows * lat_count - SHIFT_R).astype(jnp.int32).reshape(row_wins, WIN_R)
    labels = jnp.broadcast_to(
        wrapped[:, None, None, :, None], (row_wins, col_wins, levels, WIN_R, WIN_C)
    )
    labels = labels.reshape(wins, tokens)
    allowed = labels[:, :, None] == labels[:, None, :]
    scores = jnp.where(allowed[:, None], scores, jnp.float32(-1000000000.0))
    top = jnp.max(scores, axis=-1, keepdims=True)
    expo = jnp.exp(scores - top)
    probs = (expo / jnp.sum(expo, axis=-1, keepdims=True)).astype(jnp.bfloat16)
    heads_out = jnp.einsum(
        "whqk,wkhd->wqhd", probs, parts[:, :, 2], preferred_element_type=jnp.float32
    )
    heads_out = heads_out.astype(jnp.bfloat16).reshape(
        row_wins, col_wins, levels, WIN_R, WIN_C, width
    )
    heads_out = heads_out.transpose(2, 0, 3, 1, 4, 5).reshape(-1, width)
    attn = jnp.dot(heads_out, full_proj, preferred_element_type=jnp.float32).astype(jnp.bfloat16)
    attn = attn.reshape(levels, rows, cols, width)
    edges = (
        attn[:, rows - SHIFT_R :, : cols - SHIFT_C],
        attn[:, : rows - SHIFT_R, cols - SHIFT_C :],
        attn[:, rows - SHIFT_R :, cols - SHIFT_C :],
    )
    row_came, col_came, both_came = exchange(edges, 1, (), 2)
    upper = jnp.concatenate([both_came, row_came], axis=2)
    lower = jnp.concatenate([col_came, attn[:, : rows - SHIFT_R, : cols - SHIFT_C]], axis=2)
    back = jnp.concatenate([upper, lower], axis=1)
    fine_out = fine_tokens.astype(jnp.float32) + back.astype(jnp.float32)
    normed1 = layer_norm(cat_four(fine_out)).astype(jnp.bfloat16)
    if lat_count == 4 and lax.axis_size("lon") % 2 == 0:
        merged1 = in_owner_order(
            [
                jnp.dot(normed1, part, preferred_element_type=jnp.float32).astype(jnp.bfloat16)
                for part in merge_parts
            ]
        )
    else:
        merge_all = lax.all_gather(merge_one, "lat", axis=1, tiled=True)
        merged1 = jnp.dot(normed1, merge_all, preferred_element_type=jnp.float32)
        merged1 = merged1.astype(jnp.bfloat16)
    merged1 = merged1.reshape(levels, rows // 2, cols // 2, MID)
    normed2 = layer_norm(cat_four(merged1.astype(jnp.float32))).astype(jnp.bfloat16)
    pieces = coarse_apart(normed2, merge_two, mlp_in, mlp_out, split_weight)
    pieces = pieces.reshape(levels, rows // 4, cols // 4, 2, 2, MID).transpose(0, 1, 3, 2, 4, 5)
    pieces = pieces.reshape(levels, rows // 2, cols // 2, MID)
    mid_out = merged1.astype(jnp.float32) + pieces.astype(jnp.float32)
    return (fine_out, mid_out)


def on_device(
    fine_tokens, qkv_weight, proj_weight, merge_one, merge_two, mlp_in, mlp_out, split_weight
):
    levels, rows, cols, width = fine_tokens.shape
    lat_count, count = lax.axis_size("lat"), lax.axis_size("lon")
    fits = count % 4 == 0 and merge_two.shape[1] % (count * 128) == 0
    if lat_count != 4 or not fits or rows != 2 * WIN_R or cols != WIN_C or levels != 2:
        return on_any(
            fine_tokens, qkv_weight, proj_weight, merge_one, merge_two, mlp_in, mlp_out, split_weight
        )
    tokens = fine_tokens.transpose(1, 2, 0, 3).reshape(rows, cols * levels, width)
    fine, mid = whole_block(
        tokens, qkv_weight, proj_weight, merge_one, merge_two, mlp_in, mlp_out, split_weight
    )
    fine_out = fine.reshape(rows, cols, levels, width).transpose(2, 0, 1, 3)
    mid_out = mid.reshape(rows // 2, cols // 2, levels, MID).transpose(2, 0, 1, 3)
    return (fine_out, mid_out)


def solution(mesh):
    return jax.shard_map(
        on_device,
        mesh=mesh,
        in_specs=(
            P(None, "lat", "lon", None),
            P(None, "lat"),
            P(None, "lat"),
            P(None, "lat"),
            P("lon", None),
            P(None, "lon"),
            P("lon", None),
            P(None, "lon"),
        ),
        out_specs=(P(None, "lat", "lon", None), P(None, "lat", "lon", None)),
        check_vma=False,
    )
```
